32 devices in a mesh: rows: 8 (over z, x), seq: 4 (over y, core).
Axes of the slice: x: 2, y: 2, z: 4, core: 2. Of those that a mesh axis runs over, the one named last changes fastest.
Arguments:
- layer_input: bfloat16 [8, 1024, 2048], P('rows', 'seq'), may hold values from -6 to 6
- doc_lengths: int32 [8, 2], P('rows'), may hold values from 1 to 768, 1024 in all within a row
- w_qkv: bfloat16 [2048, 6144], P(('rows', 'seq')), may hold values from -0.125 to 0.125
- w_out: bfloat16 [2048, 2048], P(('rows', 'seq')), may hold values from -0.125 to 0.125
- w_gate_up: bfloat16 [2048, 16384], P(('rows', 'seq')), may hold values from -0.125 to 0.125
- w_down: bfloat16 [8192, 2048], P(('rows', 'seq')), may hold values from -0.0625 to 0.0625
- norm_gains: float32 [4, 2048], replicated, may hold values from 0.5 to 1.5
- cotangent: bfloat16 [8, 1024, 2048], P('rows', 'seq'), may hold values from -6 to 6
Outputs:
- output: bfloat16 [8, 1024, 2048], P('rows', 'seq')
- grad_input: float32 [8, 1024, 2048], P('rows', 'seq')
- grad_qkv: float32 [2048, 6144], P(('rows', 'seq'))
- grad_out: float32 [2048, 2048], P(('rows', 'seq'))
- grad_gate_up: float32 [2048, 16384], P(('rows', 'seq'))
- grad_down: float32 [8192, 2048], P(('rows', 'seq'))
- grad_gains: float32 [4, 2048], replicated
The draws below stay inside these ranges and needn't reach their ends.
Inputs may be any that keep to these rules, and one draw needn't show every extreme that they name: `doc_lengths`: each row's 2 lengths add up to 1024; no length exceeds 768.
All inputs are finite; a program needn't handle non-finite values.
Results may differ from the reference program's by a relative error of at most 0.017.
Values may be sent and summed in bfloat16 or wider, within the bound.
No kernel may reach another device: no remote copies, remote signals or barrier semaphores. Data moves between devices by JAX's collectives and lax.ppermute only.
A program may use at most 512 MiB of HBM per device.

```python
import math
import jax
import jax.numpy as jnp
import numpy as np
from jax import lax

D = 2048
H = 16
HD = 128
FF = 8192
ROW_LEN = 1024
DOCS = 2
LONGEST = 768
ROWS = 8


def shard_levels(stream_key, extent, cuts, least, largest):
    gain, own = 1.0, jax.random.fold_in(stream_key, 6)
    for position, parts in cuts:
        steps = jnp.exp(jax.random.uniform(jax.random.fold_in(own, position), (parts,), jnp.float32, least / len(cuts), largest / len(cuts)))
        gain = gain * jnp.repeat(steps, extent[position] // parts).reshape([-1 if axis == position else 1 for axis in range(len(extent))])
    return gain


def split_up(amount, total, reach, slope):
    portions = [(1 << 20) // math.isqrt(standing ** slope) + 1 for standing in range(2, amount + 1)]
    rest, holding = total - reach - (amount - 1), [1] * (amount - 1)
    while rest > 0:
        free = [i for i in range(amount - 1) if holding[i] < reach]
        pool, budget = sum([portions[i] for i in free]), rest
        for i in free:
            addition = min(reach - holding[i], max(1, budget * portions[i] // pool), rest)
            holding[i] = holding[i] + addition
            rest = rest - addition
    return np.array([reach] + holding)


def uneven_parts(stream_key, number_of, total, limit, skew):
    if number_of == 2:
        one = jax.random.randint(stream_key, (), max(1, total - limit), min(limit, total - 1) + 1)
        return jnp.stack([one, total - one])
    sizes = jnp.asarray(split_up(number_of, total, limit, skew), jnp.int32)
    couples = (number_of - 1) // 2
    source_of, receiver = sizes[1:1 + 2 * couples:2], sizes[2:2 + 2 * couples:2]
    margin = jnp.minimum(source_of - 1, limit - receiver)
    moved = jax.random.randint(jax.random.fold_in(stream_key, 1), (couples,), 0, 1 << 20) % (margin + 1)
    sizes = sizes.at[1:1 + 2 * couples:2].set(source_of - moved).at[2:2 + 2 * couples:2].set(receiver + moved)
    return sizes[jax.random.permutation(jax.random.fold_in(stream_key, 2), number_of)]


def normal_values(own_key, shape, spread, reach, pieces=(), kind=jnp.bfloat16):
    loudness = shard_levels(own_key, shape, pieces, -0.22, 0.18) if pieces else 1.0
    array = jax.random.normal(own_key, shape, jnp.float32) * spread * loudness
    return jnp.minimum(jnp.maximum(array, -reach), reach).astype(kind)


def setup_inputs(seed: int = 0) -> dict:
    key_list = jax.random.split(jax.random.key(seed), 9)
    return {
        "layer_input": normal_values(key_list[0], (ROWS, ROW_LEN, D), 1.0, 6.0, ((0, 8), (1, 4))),
        "doc_lengths": jax.vmap(lambda own: uneven_parts(own, DOCS, ROW_LEN, LONGEST, 0))(jax.random.split(key_list[1], ROWS)).reshape((ROWS, DOCS)).astype(jnp.int32),
        "w_qkv": normal_values(key_list[2], (D, 3 * D), D ** -0.5, 0.125, ((0, 32),)),
        "w_out": normal_values(key_list[3], (D, D), D ** -0.5, 0.125, ((0, 32),)),
        "w_gate_up": normal_values(key_list[4], (D, 2 * FF), D ** -0.5, 0.125, ((0, 32),)),
        "w_down": normal_values(key_list[5], (FF, D), FF ** -0.5, 0.0625, ((0, 32),)),
        "norm_gains": jnp.clip(1.0 + 0.1 * jax.random.normal(key_list[6], (4, D), jnp.float32), 0.5, 1.5),
        "cotangent": normal_values(key_list[7], (ROWS, ROW_LEN, D), 1.0, 6.0, ((0, 8), (1, 4))),
    }


@jax.custom_vjp
def low(v):
    return lax.optimization_barrier(v.astype(jnp.bfloat16)).astype(jnp.float32)

@jax.custom_vjp
def low_back(v):
    return v

def low_keep(v):
    return (low(v), None)

def low_pass(kept, grad):
    return (grad,)

def back_keep(v):
    return (v, None)

def back_low(kept, grad):
    return (low(grad),)
low.defvjp(low_keep, low_pass)
low_back.defvjp(back_keep, back_low)
eps = 1e-06
rope_base = 500000.0
highest = lax.Precision.HIGHEST

def normed(tensor, gain_row):
    return tensor * lax.rsqrt(lax.optimization_barrier(jnp.mean(tensor * tensor, axis=-1, keepdims=True)) + eps) * gain_row

def rope_tables(positions):
    half_width = HD // 2
    frequency = jnp.power(rope_base, -(jnp.arange(half_width, dtype=jnp.float32) * 2.0) / HD)
    angles = positions.astype(jnp.float32)[..., None] * frequency
    angles = jnp.concatenate([angles, angles], axis=-1)
    return (jnp.cos(angles), jnp.sin(angles))

def rotate(tensor, cosine, sine_table):
    half_width = HD // 2
    turned = jnp.concatenate([-tensor[..., half_width:], tensor[..., :half_width]], axis=-1)
    return tensor * cosine + turned * sine_table

def reference(layer_input, doc_lengths, w_qkv, w_out, w_gate_up, w_down, norm_gains, cotangent):
    doc_ends = jnp.cumsum(doc_lengths, axis=1).astype(jnp.int32)
    places = jnp.arange(ROW_LEN, dtype=jnp.int32)
    passed = (places[None, :, None] >= doc_ends[:, None, :]).astype(jnp.int32)
    segment = lax.optimization_barrier(jnp.sum(passed, axis=-1)).astype(jnp.int32)
    doc_start = lax.optimization_barrier(jnp.sum(passed * doc_lengths[:, None, :], axis=-1)).astype(jnp.int32)
    positions = places[None, :] - doc_start
    cosine, sine_table = rope_tables(positions)
    cosine = cosine[:, :, None, :]
    sine_table = sine_table[:, :, None, :]
    causal = places[:, None] >= places[None, :]
    score_scale = 1.0 / HD ** 0.5

    def attend_row(packed):
        row_q, row_k, row_v, row_seg = packed
        scores = jnp.einsum('qhd,khd->hqk', row_q, row_k, precision=highest) * score_scale
        scores = low_back(scores)
        allowed = causal & (row_seg[:, None] == row_seg[None, :])
        scores = jnp.where(allowed[None], scores, -1e+30)
        attn_probs = jax.nn.softmax(scores, axis=-1)
        return jnp.einsum('hqk,khd->qhd', low(attn_probs), row_v, precision=highest)

    def forward(inputs, weight_qkv, weight_out, weight_gu, weight_down, gains):
        tok_count = ROWS * ROW_LEN
        flat_in = inputs.reshape(tok_count, D)
        mixed_all = low_back(jnp.dot(flat_in, weight_qkv, precision=highest))
        shape4 = (ROWS, ROW_LEN, H, HD)
        queries = normed(mixed_all[:, :D], gains[0]).reshape(shape4)
        keys_all = normed(mixed_all[:, D:2 * D], gains[1]).reshape(shape4)
        queries = low(low_back(rotate(queries, cosine, sine_table)))
        keys_all = low(low_back(rotate(keys_all, cosine, sine_table)))
        values_all = low(low_back(mixed_all[:, 2 * D:].reshape(shape4)))
        attended = lax.map(jax.checkpoint(attend_row), (queries, keys_all, values_all, segment))
        attended = low(low_back(attended.reshape(tok_count, D)))
        branch = low_back(jnp.dot(attended, weight_out, precision=highest))
        hidden = flat_in + normed(branch, gains[2])
        gate_up = low_back(jnp.dot(low(hidden), weight_gu, precision=highest))
        inner = low(jax.nn.silu(gate_up[:, :FF]) * gate_up[:, FF:])
        branch2 = low_back(jnp.dot(inner, weight_down, precision=highest))
        return (hidden + normed(branch2, gains[3])).reshape(ROWS, ROW_LEN, D)
    primal = (layer_input.astype(jnp.float32), w_qkv.astype(jnp.float32), w_out.astype(jnp.float32), w_gate_up.astype(jnp.float32), w_down.astype(jnp.float32), norm_gains.astype(jnp.float32))
    result, pullback = jax.vjp(forward, *primal)
    gradients = pullback(cotangent.astype(jnp.float32))
    return (result.astype(jnp.bfloat16), gradients[0], gradients[1], gradients[2], gradients[3], gradients[4], gradients[5])
```

```python
import jax
import jax.numpy as jnp
from jax import lax
from jax.sharding import PartitionSpec as P

HD = 128
BF = jnp.bfloat16
F32 = jnp.float32

eps = 1e-06
rope_base = 500000.0


def rope_tables(positions):
    half_width = HD // 2
    frequency = jnp.power(rope_base, -(jnp.arange(half_width, dtype=F32) * 2.0) / HD)
    angles = positions.astype(F32)[:, None] * frequency
    angles = jnp.concatenate([angles, angles], axis=-1)
    return jnp.cos(angles)[:, None, :], jnp.sin(angles)[:, None, :]


def rotate(tensor, cosine, sine_table, turn_sign):
    half_width = HD // 2
    turned = jnp.concatenate([-tensor[..., half_width:], tensor[..., :half_width]], axis=-1)
    return tensor * cosine + turn_sign * turned * sine_table


def dot_nn(a, b):
    return lax.dot_general(a, b, (((1,), (0,)), ((), ())), preferred_element_type=F32)


def dot_nt(a, b):
    return lax.dot_general(a, b, (((1,), (1,)), ((), ())), preferred_element_type=F32)


def dot_tn(a, b):
    return lax.dot_general(a, b, (((0,), (0,)), ((), ())), preferred_element_type=F32)


def pick(array, index):
    return lax.dynamic_index_in_dim(array, index, 0, keepdims=False)


def after(value, *others):
    return lax.optimization_barrier((value,) + others)[0]


def norm_back(tensor, inv_scale, gain_row, upstream):
    scaled = upstream * gain_row
    average = jnp.mean(scaled * tensor, axis=-1, keepdims=True)
    grad_tensor = inv_scale * scaled - tensor * (inv_scale * inv_scale * inv_scale) * average
    gain_term = jnp.sum(upstream * tensor * inv_scale, axis=0)
    return grad_tensor, gain_term


class Comm:
    def __init__(self):
        self.rows = lax.axis_size("rows")
        self.seq = lax.axis_size("seq")
        self.zc = 4 if self.rows % 4 == 0 else self.rows
        self.xc = self.rows // self.zc
        row = lax.axis_index("rows")
        self.z, self.x = row // self.xc, row % self.xc
        self.s = lax.axis_index("seq")
        zc, xc = self.zc, self.xc
        self.zperm = [(z * xc + x, ((z + 1) % zc) * xc + x) for z in range(zc) for x in range(xc)]
        self.xperm = [(z * xc + x, z * xc + (x + 1) % xc) for z in range(zc) for x in range(xc)]

    def ring_z(self, v):
        return lax.ppermute(v, "rows", self.zperm)

    def ring_x(self, v):
        return lax.ppermute(v, "rows", self.xperm) if self.xc > 1 else v

    def swap_s(self, v, j):
        return lax.ppermute(v, "seq", [(i, i ^ j) for i in range(self.seq)])

    def zi(self, j):
        return (self.z + (self.zc - j)) % self.zc

    def xi(self, j):
        return (self.x + (self.xc - j % self.xc)) % self.xc

    def gather(self, block, x_first=False):
        n, m = block.shape
        full = jnp.zeros((self.zc, self.xc, n, m), block.dtype)

        def put(full, v, j, i):
            return lax.dynamic_update_slice(full, v[None, None], (self.zi(j), self.xi(i), 0, 0))

        zs = []
        if x_first:
            line = [block]
            for _ in range(self.xc - 1):
                line.append(self.ring_x(line[-1]))
            for j in range(self.zc):
                for i in range(self.xc):
                    full = put(full, line[i], j, i)
                if j < self.zc - 1:
                    line = [self.ring_z(v) for v in line]
                    zs.append(line[0])
        else:
            v = block
            for j in range(self.zc):
                u = v
                for i in range(self.xc):
                    full = put(full, u, j, i)
                    if i < self.xc - 1:
                        u = self.ring_x(u)
                if j < self.zc - 1:
                    v = self.ring_z(v)
                    zs.append(v)
        return full, zs

    def scatter(self, parts, z_first=False):
        zc, xc = self.zc, self.xc

        def add(moved, own):
            return moved.astype(F32) + own.astype(F32)

        if z_first:
            run = pick(parts, self.zi(1))
            for t in range(2, zc + 1):
                run = add(self.ring_z(run.astype(BF)), pick(parts, self.zi(t)))
            line = run
            run = pick(line, self.xi(1))
            for i in range(2, xc + 1):
                run = add(self.ring_x(run.astype(BF)), pick(line, self.xi(i)))
            return run

        def along_x(t):
            plane = pick(parts, self.zi(t))
            run = pick(plane, self.xi(1))
            for i in range(2, xc + 1):
                run = add(self.ring_x(run.astype(BF)), pick(plane, self.xi(i)))
            return run

        run = along_x(1)
        for t in range(2, zc + 1):
            run = add(self.ring_z(run.astype(BF)), along_x(t))
        return run

    def swap_tokens(self, v, j, axis=0):
        pieces = jnp.split(self.swap_s(v, j), self.seq, axis=axis)
        return jnp.concatenate([pieces[k ^ j] for k in range(self.seq)], axis=axis)

    def exchange(self, parts, tokens=False):
        swap = self.swap_tokens if tokens else self.swap_s
        out = parts
        for j in range(1, self.seq):
            moved = swap(pick(parts, self.s ^ j), j)
            out = lax.dynamic_update_index_in_dim(out, moved, self.s ^ j, 0)
        return out

    def gather_tokens(self, v):
        pieces = [v]
        bit = self.seq // 2
        got = {0: v}
        while bit:
            for k in sorted(got):
                got[k | bit] = self.swap_s(got[k], bit)
            bit //= 2
        return jnp.concatenate([got[k] for k in range(self.seq)], axis=0)

    def scatter_tokens(self, v):
        n = v.shape[0] // self.seq
        have = {k: v[k * n : (k + 1) * n] for k in range(self.seq)}
        bit = 1
        while bit < self.seq:
            keep = {k: have[k] for k in have if not k & bit}
            for k in sorted(keep, reverse=True):
                keep[k] = keep[k].astype(F32) + self.swap_s(have[k | bit].astype(BF), bit).astype(F32)
            have = keep
            bit *= 2
        return have[0]

    def sum_seq(self, v):
        bit = 1
        while bit < self.seq:
            v = v + self.swap_s(v, bit)
            bit *= 2
        return v

    def sum_tokens(self, v):
        bit = 1
        while bit < self.seq:
            v = v + self.swap_tokens(v, bit, 1)
            bit *= 2
        return v

    def sum_all(self, v):
        v = self.sum_seq(v)
        bit = 1
        while bit < self.rows:
            v = v + lax.ppermute(v, "rows", [(i, i ^ bit) for i in range(self.rows)])
            bit *= 2
        return v


def per_device(layer_input, doc_lengths, w_qkv, w_out, w_gate_up, w_down, norm_gains, cotangent):
    c = Comm()
    rows, seq, s = c.rows, c.seq, c.s
    _, tl, d = layer_input.shape
    toks = tl * seq
    heads = d // HD
    hl = heads // seq
    wide = hl * HD
    n_in, n_out, n_ff = w_qkv.shape[0], w_out.shape[0], w_down.shape[0]
    ff = n_ff * rows
    flat_in = layer_input.reshape(tl, d)
    pairs = n_out * seq == 2 * HD and seq == 4 and hl == rows // 2

    if pairs:
        send_qkv = w_qkv.reshape(n_in, 3, 2, hl, 2, HD).transpose(4, 2, 0, 1, 3, 5)
    else:
        send_qkv = w_qkv.reshape(n_in, 3, seq, wide).transpose(2, 0, 1, 3)
    slab_qkv = c.exchange(send_qkv.reshape(seq, n_in, 3 * wide)).reshape(seq * n_in, 3 * wide)
    send_gu = w_gate_up.reshape(n_in, 2, rows, seq, n_ff).transpose(3, 0, 1, 2, 4)
    slab_gu = c.exchange(send_gu.reshape(seq, n_in, 2 * ff)).reshape(seq * n_in, 2 * ff)
    x_full = c.gather_tokens(flat_in)

    full_qkv, z_qkv = c.gather(slab_qkv)
    full_qkv = full_qkv.reshape(d, 3 * wide)
    full_out, z_out = c.gather(w_out)
    full_out = full_out.reshape(wide, d)
    half = d // 2
    down_a, z_a = c.gather(after(w_down[:, :half], z_qkv[0]), True)
    full_gu, z_gu = c.gather(after(slab_gu, z_qkv[-1]))
    full_gu = full_gu.reshape(d, 2 * ff)
    down_b, z_b = c.gather(after(w_down[:, half:], z_gu[0]))
    full_down = jnp.concatenate([down_a.reshape(ff, half), down_b.reshape(ff, d - half)], axis=1)

    doc_ends = jnp.cumsum(doc_lengths, axis=1)[0]
    lengths = doc_lengths[0]
    places = jnp.concatenate(
        [(s ^ j) * tl + jnp.arange(tl, dtype=jnp.int32) for j in range(seq)]
    )
    passed = (places[:, None] >= doc_ends[None, :]).astype(jnp.int32)
    segment = jnp.sum(passed, axis=-1)
    positions = places - jnp.sum(passed * lengths[None, :], axis=-1)
    cosine, sine_table = rope_tables(positions)
    allowed = (places[:, None] >= places[None, :]) & (segment[:, None] == segment[None, :])
    if pairs:
        gains4 = norm_gains.reshape(4, 2, hl, 2, HD).transpose(3, 1, 0, 2, 4).reshape(seq, 4, wide)
    else:
        gains4 = norm_gains.reshape(4, seq, wide).transpose(1, 0, 2)
    gains_own = pick(gains4, s)

    mixed = dot_nn(x_full, full_qkv)
    query_pre, key_pre = mixed[:, :wide], mixed[:, wide : 2 * wide]
    squares = jnp.stack([jnp.sum(query_pre * query_pre, -1), jnp.sum(key_pre * key_pre, -1)])
    scales = lax.rsqrt(c.sum_tokens(squares) / d + eps)
    query_scale, key_scale = scales[0][:, None], scales[1][:, None]
    shape3 = (toks, hl, HD)
    query = rotate((query_pre * query_scale * gains_own[0]).reshape(shape3), cosine, sine_table, 1.0)
    key = rotate((key_pre * key_scale * gains_own[1]).reshape(shape3), cosine, sine_table, 1.0)
    query, key = query.astype(BF), key.astype(BF)
    value = mixed[:, 2 * wide :].reshape(shape3).astype(BF)
    score_scale = 1.0 / HD**0.5
    scores = jnp.einsum("qhd,khd->hqk", query, key, preferred_element_type=F32) * score_scale
    scores = jnp.where(allowed[None], scores, -1e30)
    row_max = jnp.max(scores, axis=-1, keepdims=True)
    exponent = jnp.exp(scores - row_max)
    probs = exponent / jnp.sum(exponent, axis=-1, keepdims=True)
    probs_low = probs.astype(BF)
    attended = jnp.einsum("hqk,khd->qhd", probs_low, value, preferred_element_type=F32).astype(BF)

    def to_out(v):
        if pairs:
            core = s % 2
            v = v.reshape(toks, hl, 2, HD // 2).transpose(2, 0, 1, 3).reshape(2, toks, wide // 2)
            own, got = pick(v, core), c.swap_tokens(pick(v, 1 - core), 1)
            first = jnp.where(core == 0, own, got)
            second = jnp.where(core == 0, got, own)
            return jnp.concatenate([first, second], axis=1)
        v = v.reshape(toks, wide // (seq * n_out), seq, n_out)
        v = c.exchange(v.transpose(2, 0, 1, 3).reshape(seq, toks, wide // seq), True)
        return v.transpose(1, 0, 2).reshape(toks, wide)

    def from_out(v):
        if pairs:
            core = s % 2
            v = v.reshape(toks, 2, wide // 2).transpose(1, 0, 2)
            own, got = pick(v, core), c.swap_tokens(pick(v, 1 - core), 1)
            first = jnp.where(core == 0, own, got).reshape(toks, hl, 1, HD // 2)
            second = jnp.where(core == 0, got, own).reshape(toks, hl, 1, HD // 2)
            return jnp.concatenate([first, second], axis=2).reshape(shape3)
        v = c.exchange(v.reshape(toks, seq, wide // seq).transpose(1, 0, 2), True)
        v = v.reshape(seq, toks, wide // (seq * n_out), n_out).transpose(1, 2, 0, 3)
        return v.reshape(shape3)

    attended = to_out(attended)
    branch = c.scatter_tokens(dot_nn(attended, full_out))
    branch_scale = lax.rsqrt(jnp.mean(branch * branch, axis=-1, keepdims=True) + eps)
    hidden = flat_in.astype(F32) + branch * branch_scale * norm_gains[2]
    hidden_low = c.gather_tokens(hidden.astype(BF))

    gate_up = dot_nn(hidden_low, full_gu)
    gate, up = gate_up[:, :ff], gate_up[:, ff:]
    sig = jax.nn.sigmoid(gate)
    silu_gate = gate * sig
    inner = (silu_gate * up).astype(BF)
    branch2 = c.scatter_tokens(dot_nn(inner, full_down))
    branch2_scale = lax.rsqrt(jnp.mean(branch2 * branch2, axis=-1, keepdims=True) + eps)
    output = (hidden + branch2 * branch2_scale * norm_gains[3]).astype(BF)

    upstream = cotangent.reshape(tl, d).astype(F32)
    grad_branch2, gain_mlp = norm_back(branch2, branch2_scale, norm_gains[3], upstream)
    grad_branch2 = c.gather_tokens(grad_branch2.astype(BF))
    zx = (c.zc, c.xc)
    g_down = dot_tn(inner, grad_branch2).astype(BF)
    sum_a = c.scatter(g_down[:, :half].reshape(zx + (n_ff, half)), True)
    sum_b = c.scatter(g_down[:, half:].reshape(zx + (n_ff, d - half)))
    grad_down = jnp.concatenate([sum_a, sum_b], axis=1)
    grad_inner = dot_nt(grad_branch2, full_down)
    grad_gate = grad_inner * up * sig * (1.0 + gate * (1.0 - sig))
    grad_gu = jnp.concatenate([grad_gate, grad_inner * silu_gate], axis=1).astype(BF)
    g_gu = dot_tn(hidden_low, grad_gu).astype(BF)
    sum_gu = c.scatter(g_gu.reshape(zx + (seq * n_in, 2 * ff)))
    grad_hidden = upstream + c.scatter_tokens(dot_nt(grad_gu, full_gu))
    grad_branch, gain_attn = norm_back(branch, branch_scale, norm_gains[2], grad_hidden)
    grad_branch = c.gather_tokens(grad_branch.astype(BF))
    g_out = dot_tn(attended, grad_branch).astype(BF)
    grad_out = c.scatter(g_out.reshape(zx + (n_out, d)))
    grad_att = from_out(dot_nt(grad_branch, full_out).astype(BF))
    grad_probs = jnp.einsum("qhd,khd->hqk", grad_att, value, preferred_element_type=F32)
    grad_value = jnp.einsum("hqk,qhd->khd", probs_low, grad_att, preferred_element_type=F32)
    row_sum = jnp.sum(probs * grad_probs, axis=-1, keepdims=True)
    grad_scores = (probs * (grad_probs - row_sum)).astype(BF)
    grad_query = jnp.einsum("hqk,khd->qhd", grad_scores, key, preferred_element_type=F32)
    grad_key = jnp.einsum("hqk,qhd->khd", grad_scores, query, preferred_element_type=F32)
    grad_query = (grad_query * score_scale).astype(BF).astype(F32)
    grad_key = (grad_key * score_scale).astype(BF).astype(F32)
    e_query = rotate(grad_query, cosine, sine_table, -1.0).reshape(toks, wide)
    e_key = rotate(grad_key, cosine, sine_table, -1.0).reshape(toks, wide)
    scaled_q, scaled_k = e_query * gains_own[0], e_key * gains_own[1]
    means = c.sum_tokens(
        jnp.stack([jnp.sum(scaled_q * query_pre, -1), jnp.sum(scaled_k * key_pre, -1)])
    )
    means = means / d
    grad_qp = query_scale * scaled_q - query_pre * query_scale**3 * means[0][:, None]
    grad_kp = key_scale * scaled_k - key_pre * key_scale**3 * means[1][:, None]
    gain_query = jnp.sum(e_query * query_pre * query_scale, axis=0)
    gain_key = jnp.sum(e_key * key_pre * key_scale, axis=0)
    grad_mixed = jnp.concatenate(
        [grad_qp.astype(BF), grad_kp.astype(BF), grad_value.astype(BF).reshape(toks, wide)], axis=1
    )
    g_qkv = dot_tn(x_full, grad_mixed).astype(BF)
    sum_qkv = c.scatter(g_qkv.reshape(zx + (seq * n_in, 3 * wide)))
    grad_input = grad_hidden + c.scatter_tokens(dot_nt(grad_mixed, full_qkv))

    back_gu = c.exchange(sum_gu.astype(BF).reshape(seq, n_in, 2 * ff)).astype(F32)
    grad_gate_up = back_gu.reshape(seq, n_in, 2, rows, n_ff).transpose(1, 2, 3, 0, 4)
    back_qkv = c.exchange(sum_qkv.astype(BF).reshape(seq, n_in, 3 * wide)).astype(F32)
    if pairs:
        grad_qkv = back_qkv.reshape(2, 2, n_in, 3, hl, HD).transpose(2, 3, 1, 4, 0, 5)
    else:
        grad_qkv = back_qkv.reshape(seq, n_in, 3, wide).transpose(1, 2, 0, 3)

    own_terms = jnp.zeros((seq, 2, wide), F32)
    own_terms = lax.dynamic_update_slice(own_terms, jnp.stack([gain_query, gain_key])[None], (s, 0, 0))
    if pairs:
        own_terms = own_terms.reshape(2, 2, 2, hl, HD).transpose(2, 1, 3, 0, 4)
    else:
        own_terms = own_terms.transpose(1, 0, 2)
    terms = jnp.concatenate([own_terms.reshape(2, d), jnp.stack([gain_attn, gain_mlp])])
    grad_gains = c.sum_all(terms)

    return (
        output.reshape(layer_input.shape),
        grad_input.reshape(layer_input.shape),
        grad_qkv.reshape(w_qkv.shape),
        grad_out,
        grad_gate_up.reshape(w_gate_up.shape),
        grad_down,
        grad_gains,
    )


def solution(mesh):
    both = P(("rows", "seq"), None)
    tokens = P("rows", "seq", None)
    return jax.shard_map(
        per_device,
        mesh=mesh,
        in_specs=(tokens, P("rows", None), both, both, both, both, P(), tokens),
        out_specs=(tokens, tokens, both, both, both, both, P()),
        check_vma=False,
    )
```

```python
import jax
import jax.numpy as jnp
from jax import lax
from jax.sharding import PartitionSpec as P

HD = 128
BF = jnp.bfloat16
F32 = jnp.float32

eps = 1e-06
rope_base = 500000.0


def rope_tables(positions):
    half_width = HD // 2
    frequency = jnp.power(rope_base, -(jnp.arange(half_width, dtype=F32) * 2.0) / HD)
    angles = positions.astype(F32)[:, None] * frequency
    angles = jnp.concatenate([angles, angles], axis=-1)
    return jnp.cos(angles)[:, None, :], jnp.sin(angles)[:, None, :]


def rotate(tensor, cosine, sine_table, turn_sign):
    half_width = HD // 2
    turned = jnp.concatenate([-tensor[..., half_width:], tensor[..., :half_width]], axis=-1)
    return tensor * cosine + turn_sign * turned * sine_table


def dot_nn(a, b):
    return lax.dot_general(a, b, (((1,), (0,)), ((), ())), preferred_element_type=F32)


def dot_nt(a, b):
    return lax.dot_general(a, b, (((1,), (1,)), ((), ())), preferred_element_type=F32)


def dot_tn(a, b):
    return lax.dot_general(a, b, (((0,), (0,)), ((), ())), preferred_element_type=F32)


def pick(array, index):
    return lax.dynamic_index_in_dim(array, index, 0, keepdims=False)


def after(value, *others):
    return lax.optimization_barrier((value,) + others)[0]


def norm_back(tensor, inv_scale, gain_row, upstream):
    scaled = upstream * gain_row
    average = jnp.mean(scaled * tensor, axis=-1, keepdims=True)
    grad_tensor = inv_scale * scaled - tensor * (inv_scale * inv_scale * inv_scale) * average
    gain_term = jnp.sum(upstream * tensor * inv_scale, axis=0)
    return grad_tensor, gain_term


class Comm:
    def __init__(self, group=8):
        rows, seq = lax.axis_size("rows"), lax.axis_size("seq")
        self.part = max(1, min(rows, group // seq))
        self.copies, self.size, self.count = rows // self.part, self.part * seq, rows * seq
        row, s = lax.axis_index("rows"), lax.axis_index("seq")
        self.d = row // self.part
        self.g = (row % self.part) * seq + s
        self.seq, self.t, self.s = seq, row % self.part, s
        bits = [1 << i for i in range(self.size.bit_length() - 1)]
        self.bits = bits
        self.order = list(range(0, self.size, 2)) + list(range(1, self.size, 2))

    def send(self, v, pairs):
        return lax.ppermute(v, ("rows", "seq"), pairs)

    def swap(self, v, j):
        return self.send(v, [(i, i ^ j) for i in range(self.count)])

    def ring(self, v):
        return self.send(v, [(i, (i + self.size) % self.count) for i in range(self.count)])

    def near(self, j):
        return (self.d + (self.copies - j)) % self.copies

    def gather(self, block, firsts=()):
        full = jnp.zeros((self.copies,) + block.shape, block.dtype)
        arrivals = []
        for j in range(self.copies):
            full = lax.dynamic_update_index_in_dim(full, block, self.near(j), 0)
            if j < self.copies - 1:
                if j < len(firsts):
                    block = after(block, firsts[j])
                block = self.ring(block)
                arrivals.append(block)
        return full, arrivals

    def scatter(self, parts):
        run = pick(parts, self.near(1))
        for j in range(2, self.copies + 1):
            run = self.ring(run.astype(BF)).astype(F32) + pick(parts, self.near(j)).astype(F32)
        return run

    def exchange(self, parts, tokens=False):
        swap = self.swap_tokens if tokens else self.swap
        for bit in self.bits:
            own = (self.g // bit) % 2
            shape = parts.shape
            parts = parts.reshape((self.size // (2 * bit), 2, bit) + shape[1:])
            other = lax.dynamic_index_in_dim(parts, 1 - own, 1, keepdims=False)
            axis = 2 if tokens else 0
            moved = swap(other, bit, axis) if tokens else swap(other, bit)
            parts = lax.dynamic_update_index_in_dim(parts, moved, 1 - own, 1).reshape(shape)
        return parts

    def swap_tokens(self, v, j, axis=0):
        pieces = jnp.split(self.swap(v, j), self.size, axis=axis)
        place = {k: p for p, k in enumerate(self.order)}
        return jnp.concatenate([pieces[place[k ^ j]] for k in self.order], axis=axis)

    def gather_tokens(self, v):
        got = {0: v}
        if self.size == 8:
            half = v.shape[0] // 2
            got[4], got[2] = self.swap(v, 4), self.swap(v, 2)
            got[1] = self.swap(v, 1)
            got[6] = jnp.concatenate([self.swap(got[4][:half], 2), self.swap(got[2][half:], 4)], axis=0)
            for k in (2, 4, 6):
                got[k + 1] = self.swap(got[k], 1)
        else:
            for bit in self.bits[::-1]:
                for k in sorted(got):
                    got[k | bit] = self.swap(got[k], bit)
        return jnp.concatenate([got[k] for k in self.order], axis=0)

    def scatter_tokens(self, tokens, make_dot):
        n = tokens.shape[0] // 2
        away = make_dot(tokens[n:]).astype(BF)
        m = n // (self.size // 2)
        moved = [self.swap(away[k * m : (k + 1) * m], 1) for k in range(self.size // 2)]
        kept = make_dot(tokens[:n])
        have = {2 * k: kept[k * m : (k + 1) * m] + moved[k].astype(F32) for k in range(self.size // 2)}
        if self.size == 8:
            half = m // 2
            last = have[6].astype(BF)
            four, two = self.swap(last[half:], 2), self.swap(last[:half], 4)
            mid4, mid2 = have[4].astype(BF), have[2].astype(BF)
            add4 = (have[4][half:] + four.astype(F32)).astype(BF)
            add2 = (have[2][:half] + two.astype(F32)).astype(BF)
            a = jnp.concatenate([self.swap(mid4[:half], 4), self.swap(add4, 4)], axis=0)
            b = jnp.concatenate([self.swap(add2, 2), self.swap(mid2[half:], 2)], axis=0)
            return have[0] + a.astype(F32) + b.astype(F32)
        for bit in self.bits[1:]:
            for k in [k for k in have if k & bit]:
                have[k ^ bit] = have[k ^ bit] + self.swap(have.pop(k).astype(BF), bit).astype(F32)
        return have[0]

    def sum_tokens(self, v):
        for bit in self.bits:
            v = v + self.swap_tokens(v, bit, 1)
        return v

    def sum_all(self, v):
        bit = 1
        while bit < self.count:
            v = v + self.swap(v, bit)
            bit *= 2
        return v


def per_device(layer_input, doc_lengths, w_qkv, w_out, w_gate_up, w_down, norm_gains, cotangent):
    c = Comm()
    copies, size, part = c.copies, c.size, c.part
    _, tl, d = layer_input.shape
    toks, row_len = tl * size, tl * c.seq
    heads = d // HD
    hl = heads // size
    wide = hl * HD
    n_in, n_out, n_ff = w_qkv.shape[0], w_out.shape[0], w_down.shape[0]
    chunks = 2
    piece = n_ff // chunks
    ffc = piece * copies
    flat_in = layer_input.reshape(tl, d)
    pairs = 2 * n_out == HD and 2 * hl == copies
    half_group = size // 2

    x_full = c.gather_tokens(flat_in)
    if pairs:
        send_qkv = w_qkv.reshape(n_in, 3, 2, hl, half_group, HD).transpose(4, 2, 0, 1, 3, 5)
    else:
        send_qkv = w_qkv.reshape(n_in, 3, size, wide).transpose(2, 0, 1, 3)
    slab_qkv = c.exchange(send_qkv.reshape(size, n_in, 3 * wide)).reshape(size * n_in, 3 * wide)
    send_gu = w_gate_up.reshape(n_in, 2, copies, size, chunks, piece).transpose(3, 4, 0, 1, 2, 5)
    slab_gu = c.exchange(send_gu.reshape(size, chunks, n_in, 2 * ffc))

    full_out, _ = c.gather(w_out)
    full_out = full_out.reshape(wide, d)
    full_qkv, z_qkv = c.gather(slab_qkv)
    full_qkv = full_qkv.reshape(d, 3 * wide)
    full_gu, full_down, last = [], [], z_qkv
    for k in range(chunks):
        full, last = c.gather(slab_gu[:, k].reshape(size * n_in, 2 * ffc), last[-2:])
        full_gu.append(full.reshape(d, 2 * ffc))
    for k in range(chunks):
        full, last = c.gather(w_down[k * piece : (k + 1) * piece], last[-2:])
        full_down.append(full.reshape(ffc, d))
    full_down = jnp.concatenate(full_down, axis=0)

    lengths = doc_lengths.astype(jnp.int32)
    other = [lengths]
    for j in range(1, part):
        other.append(c.swap(lengths, j * c.seq))
    lengths = jnp.concatenate(other, axis=0)
    doc_ends = jnp.cumsum(lengths, axis=1)
    near = [k % c.seq for k in c.order if k < c.seq]
    places = jnp.concatenate([(c.s ^ k) * tl + jnp.arange(tl, dtype=jnp.int32) for k in near])
    passed = (places[None, :, None] >= doc_ends[:, None, :]).astype(jnp.int32)
    segment = jnp.sum(passed, axis=-1)
    positions = places[None, :] - jnp.sum(passed * lengths[:, None, :], axis=-1)
    allowed = (places[:, None] >= places[None, :])[None] & (segment[:, :, None] == segment[:, None, :])

    def by_rows(v):
        v = v.reshape((2, part, c.seq // 2, tl) + v.shape[1:])
        return v.swapaxes(0, 1).reshape((part, row_len) + v.shape[4:])

    def by_tokens(v):
        v = v.reshape((part, 2, c.seq // 2, tl) + v.shape[2:])
        return v.swapaxes(0, 1).reshape((toks,) + v.shape[4:])

    cosine, sine_table = rope_tables(by_tokens(positions))
    if pairs:
        gains4 = norm_gains.reshape(4, 2, hl, half_group, HD).transpose(3, 1, 0, 2, 4).reshape(size, 4, wide)
    else:
        gains4 = norm_gains.reshape(4, size, wide).transpose(1, 0, 2)
    gains_own = pick(gains4, c.g)

    mixed = dot_nn(x_full, full_qkv)
    query_pre, key_pre = mixed[:, :wide], mixed[:, wide : 2 * wide]
    squares = jnp.stack([jnp.sum(query_pre * query_pre, -1), jnp.sum(key_pre * key_pre, -1)])
    scales = lax.rsqrt(c.sum_tokens(squares) / d + eps)
    query_scale, key_scale = scales[0][:, None], scales[1][:, None]
    shape3 = (toks, hl, HD)
    query = rotate((query_pre * query_scale * gains_own[0]).reshape(shape3), cosine, sine_table, 1.0)
    key = rotate((key_pre * key_scale * gains_own[1]).reshape(shape3), cosine, sine_table, 1.0)
    query, key = by_rows(query.astype(BF)), by_rows(key.astype(BF))
    value = by_rows(mixed[:, 2 * wide :].reshape(shape3).astype(BF))
    score_scale = 1.0 / HD**0.5
    scores = jnp.einsum("rqhd,rkhd->rhqk", query, key, preferred_element_type=F32) * score_scale
    scores = jnp.where(allowed[:, None], scores, -1e30)
    row_max = jnp.max(scores, axis=-1, keepdims=True)
    exponent = jnp.exp(scores - row_max)
    probs = exponent / jnp.sum(exponent, axis=-1, keepdims=True)
    probs_low = probs.astype(BF)
    attended = jnp.einsum("rhqk,rkhd->rqhd", probs_low, value, preferred_element_type=F32).astype(BF)

    def to_out(v):
        if pairs:
            core = c.g % 2
            v = v.reshape(toks, hl, 2, HD // 2).transpose(2, 0, 1, 3).reshape(2, toks, wide // 2)
            own, got = pick(v, core), c.swap_tokens(pick(v, 1 - core), 1)
            first = jnp.where(core == 0, own, got)
            second = jnp.where(core == 0, got, own)
            return jnp.concatenate([first, second], axis=1)
        v = v.reshape(toks, wide // (size * n_out), size, n_out)
        v = c.exchange(v.transpose(2, 0, 1, 3).reshape(size, toks, wide // size), True)
        return v.transpose(1, 0, 2).reshape(toks, wide)

    def from_out(v):
        if pairs:
            core = c.g % 2
            v = v.reshape(toks, 2, wide // 2).transpose(1, 0, 2)
            own, got = pick(v, core), c.swap_tokens(pick(v, 1 - core), 1)
            first = jnp.where(core == 0, own, got).reshape(toks, hl, 1, HD // 2)
            second = jnp.where(core == 0, got, own).reshape(toks, hl, 1, HD // 2)
            return jnp.concatenate([first, second], axis=2).reshape(shape3)
        v = c.exchange(v.reshape(toks, size, wide // size).transpose(1, 0, 2), True)
        v = v.reshape(size, toks, wide // (size * n_out), n_out).transpose(1, 2, 0, 3)
        return v.reshape(shape3)

    attended = to_out(by_tokens(attended))
    branch = c.scatter_tokens(attended, lambda v: dot_nn(v, full_out))
    branch_scale = lax.rsqrt(jnp.mean(branch * branch, axis=-1, keepdims=True) + eps)
    hidden = flat_in.astype(F32) + branch * branch_scale * norm_gains[2]
    hidden_low = c.gather_tokens(hidden.astype(BF))

    gates, ups, inners = [], [], []
    for k in range(chunks):
        gate_up = dot_nn(hidden_low, full_gu[k])
        gate, up = gate_up[:, :ffc], gate_up[:, ffc:]
        gates.append(gate)
        ups.append(up)
        inners.append((gate * jax.nn.sigmoid(gate) * up).astype(BF))
    inner = jnp.concatenate(inners, axis=1)
    branch2 = c.scatter_tokens(inner, lambda v: dot_nn(v, full_down))
    branch2_scale = lax.rsqrt(jnp.mean(branch2 * branch2, axis=-1, keepdims=True) + eps)
    output = (hidden + branch2 * branch2_scale * norm_gains[3]).astype(BF)

    upstream = cotangent.reshape(tl, d).astype(F32)
    grad_branch2, gain_mlp = norm_back(branch2, branch2_scale, norm_gains[3], upstream)
    grad_branch2 = c.gather_tokens(grad_branch2.astype(BF))
    sums_down, sums_gu, grads_gu = [], [], []
    for k in range(chunks):
        g_down = dot_tn(inners[k], grad_branch2).astype(BF)
        sums_down.append(c.scatter(g_down.reshape(copies, piece, d)))
    for k in range(chunks):
        gate, up = gates[k], ups[k]
        sig = jax.nn.sigmoid(gate)
        grad_inner = dot_nt(grad_branch2, full_down[k * ffc : (k + 1) * ffc])
        grad_gate = grad_inner * up * sig * (1.0 + gate * (1.0 - sig))
        grad_gu = jnp.concatenate([grad_gate, grad_inner * (gate * sig)], axis=1).astype(BF)
        grads_gu.append(grad_gu)
        g_gu = dot_tn(hidden_low, grad_gu).astype(BF)
        sums_gu.append(c.scatter(g_gu.reshape(copies, size * n_in, 2 * ffc)))
    grad_gu = jnp.concatenate(grads_gu, axis=1)
    full_gu = jnp.concatenate(full_gu, axis=1)
    grad_hidden = upstream + c.scatter_tokens(grad_gu, lambda v: dot_nt(v, full_gu))
    grad_branch, gain_attn = norm_back(branch, branch_scale, norm_gains[2], grad_hidden)
    grad_branch = c.gather_tokens(grad_branch.astype(BF))
    g_out = dot_tn(attended, grad_branch).astype(BF)
    grad_out = c.scatter(g_out.reshape(copies, n_out, d))
    grad_att = by_rows(from_out(dot_nt(grad_branch, full_out).astype(BF)))
    grad_probs = jnp.einsum("rqhd,rkhd->rhqk", grad_att, value, preferred_element_type=F32)
    grad_value = jnp.einsum("rhqk,rqhd->rkhd", probs_low, grad_att, preferred_element_type=F32)
    row_sum = jnp.sum(probs * grad_probs, axis=-1, keepdims=True)
    grad_scores = (probs * (grad_probs - row_sum)).astype(BF)
    grad_query = jnp.einsum("rhqk,rkhd->rqhd", grad_scores, key, preferred_element_type=F32)
    grad_key = jnp.einsum("rhqk,rqhd->rkhd", grad_scores, query, preferred_element_type=F32)
    grad_query = by_tokens((grad_query * score_scale).astype(BF)).astype(F32)
    grad_key = by_tokens((grad_key * score_scale).astype(BF)).astype(F32)
    grad_value = by_tokens(grad_value.astype(BF)).reshape(toks, wide)
    e_query = rotate(grad_query, cosine, sine_table, -1.0).reshape(toks, wide)
    e_key = rotate(grad_key, cosine, sine_table, -1.0).reshape(toks, wide)
    scaled_q, scaled_k = e_query * gains_own[0], e_key * gains_own[1]
    means = c.sum_tokens(
        jnp.stack([jnp.sum(scaled_q * query_pre, -1), jnp.sum(scaled_k * key_pre, -1)])
    )
    means = means / d
    grad_qp = query_scale * scaled_q - query_pre * query_scale**3 * means[0][:, None]
    grad_kp = key_scale * scaled_k - key_pre * key_scale**3 * means[1][:, None]
    gain_query = jnp.sum(e_query * query_pre * query_scale, axis=0)
    gain_key = jnp.sum(e_key * key_pre * key_scale, axis=0)
    grad_mixed = jnp.concatenate([grad_qp.astype(BF), grad_kp.astype(BF), grad_value], axis=1)
    g_qkv = dot_tn(x_full, grad_mixed).astype(BF)
    sum_qkv = c.scatter(g_qkv.reshape(copies, size * n_in, 3 * wide))
    grad_input = grad_hidden + c.scatter_tokens(grad_mixed, lambda v: dot_nt(v, full_qkv))

    back_gu = jnp.stack([v.astype(BF).reshape(size, n_in, 2 * ffc) for v in sums_gu], axis=1)
    back_gu = c.exchange(back_gu).astype(F32)
    back_gu = back_gu.reshape(size, chunks, n_in, 2, copies, piece)
    grad_gate_up = back_gu.transpose(2, 3, 4, 0, 1, 5)
    back_qkv = c.exchange(sum_qkv.astype(BF).reshape(size, n_in, 3 * wide)).astype(F32)
    if pairs:
        grad_qkv = back_qkv.reshape(half_group, 2, n_in, 3, hl, HD).transpose(2, 3, 1, 4, 0, 5)
    else:
        grad_qkv = back_qkv.reshape(size, n_in, 3, wide).transpose(1, 2, 0, 3)

    own_terms = jnp.zeros((size, 2, wide), F32)
    own_terms = lax.dynamic_update_slice(own_terms, jnp.stack([gain_query, gain_key])[None], (c.g, 0, 0))
    if pairs:
        own_terms = own_terms.reshape(half_group, 2, 2, hl, HD).transpose(2, 1, 3, 0, 4)
    else:
        own_terms = own_terms.transpose(1, 0, 2)
    terms = jnp.concatenate([own_terms.reshape(2, d), jnp.stack([gain_attn, gain_mlp])])
    grad_gains = c.sum_all(terms)

    return (
        output.reshape(layer_input.shape),
        grad_input.reshape(layer_input.shape),
        grad_qkv.reshape(w_qkv.shape),
        grad_out,
        grad_gate_up.reshape(w_gate_up.shape),
        jnp.concatenate(sums_down, axis=0),
        grad_gains,
    )


def solution(mesh):
    both = P(("rows", "seq"), None)
    tokens = P("rows", "seq", None)
    return jax.shard_map(
        per_device,
        mesh=mesh,
        in_specs=(tokens, P("rows", None), both, both, both, both, P(), tokens),
        out_specs=(tokens, tokens, both, both, both, both, P()),
        check_vma=False,
    )
```

```python
import jax
import jax.numpy as jnp
from jax import lax
from jax.sharding import PartitionSpec as P

HD = 128
BF = jnp.bfloat16
F32 = jnp.float32

eps = 1e-06
rope_base = 500000.0


def rope_tables(positions):
    half_width = HD // 2
    frequency = jnp.power(rope_base, -(jnp.arange(half_width, dtype=F32) * 2.0) / HD)
    angles = positions.astype(F32)[:, None] * frequency
    angles = jnp.concatenate([angles, angles], axis=-1)
    return jnp.cos(angles)[:, None, :], jnp.sin(angles)[:, None, :]


def rotate(tensor, cosine, sine_table, turn_sign):
    half_width = HD // 2
    turned = jnp.concatenate([-tensor[..., half_width:], tensor[..., :half_width]], axis=-1)
    return tensor * cosine + turn_sign * turned * sine_table


def dot_nn(a, b):
    return lax.dot_general(a, b, (((1,), (0,)), ((), ())), preferred_element_type=F32)


def dot_nt(a, b):
    return lax.dot_general(a, b, (((1,), (1,)), ((), ())), preferred_element_type=F32)


def dot_tn(a, b):
    return lax.dot_general(a, b, (((0,), (0,)), ((), ())), preferred_element_type=F32)


def pick(array, index):
    return lax.dynamic_index_in_dim(array, index, 0, keepdims=False)


def after(value, *others):
    return lax.optimization_barrier((value,) + others)[0]


def norm_back(tensor, inv_scale, gain_row, upstream):
    scaled = upstream * gain_row
    average = jnp.mean(scaled * tensor, axis=-1, keepdims=True)
    grad_tensor = inv_scale * scaled - tensor * (inv_scale * inv_scale * inv_scale) * average
    gain_term = jnp.sum(upstream * tensor * inv_scale, axis=0)
    return grad_tensor, gain_term


class Comm:
    def __init__(self, group=8):
        rows, seq = lax.axis_size("rows"), lax.axis_size("seq")
        self.part = max(1, min(rows, group // seq))
        self.copies, self.size, self.count = rows // self.part, self.part * seq, rows * seq
        row, s = lax.axis_index("rows"), lax.axis_index("seq")
        self.d = row // self.part
        self.g = (row % self.part) * seq + s
        self.seq, self.t, self.s = seq, row % self.part, s
        bits = [1 << i for i in range(self.size.bit_length() - 1)]
        self.bits = bits
        self.lines = [[i * self.size + g for i in range(self.copies)] for g in range(self.size)]
        self.order = list(range(0, self.size, 2)) + list(range(1, self.size, 2))

    def send(self, v, pairs):
        return lax.ppermute(v, ("rows", "seq"), pairs)

    def swap(self, v, j):
        return self.send(v, [(i, i ^ j) for i in range(self.count)])

    def gather(self, block):
        return lax.all_gather(block, ("rows", "seq"), axis=0, tiled=True, axis_index_groups=self.lines)

    def scatter(self, parts):
        return lax.psum_scatter(
            parts, ("rows", "seq"), scatter_dimension=0, tiled=True, axis_index_groups=self.lines
        )

    def exchange(self, parts, tokens=False):
        swap = self.swap_tokens if tokens else self.swap
        for bit in self.bits:
            own = (self.g // bit) % 2
            shape = parts.shape
            parts = parts.reshape((self.size // (2 * bit), 2, bit) + shape[1:])
            other = lax.dynamic_index_in_dim(parts, 1 - own, 1, keepdims=False)
            axis = 2 if tokens else 0
            moved = swap(other, bit, axis) if tokens else swap(other, bit)
            parts = lax.dynamic_update_index_in_dim(parts, moved, 1 - own, 1).reshape(shape)
        return parts

    def swap_tokens(self, v, j, axis=0):
        pieces = jnp.split(self.swap(v, j), self.size, axis=axis)
        place = {k: p for p, k in enumerate(self.order)}
        return jnp.concatenate([pieces[place[k ^ j]] for k in self.order], axis=axis)

    def gather_tokens(self, v):
        got = {0: v}
        if self.size == 8:
            half = v.shape[0] // 2
            got[4], got[2] = self.swap(v, 4), self.swap(v, 2)
            got[1] = self.swap(v, 1)
            got[6] = jnp.concatenate([self.swap(got[4][:half], 2), self.swap(got[2][half:], 4)], axis=0)
            for k in (2, 4, 6):
                got[k + 1] = self.swap(got[k], 1)
        else:
            for bit in self.bits[::-1]:
                for k in sorted(got):
                    got[k | bit] = self.swap(got[k], bit)
        return jnp.concatenate([got[k] for k in self.order], axis=0)

    def scatter_tokens(self, tokens, make_dot):
        n = tokens.shape[0] // 2
        away = make_dot(tokens[n:]).astype(BF)
        m = n // (self.size // 2)
        moved = [self.swap(away[k * m : (k + 1) * m], 1) for k in range(self.size // 2)]
        kept = make_dot(tokens[:n])
        have = {2 * k: kept[k * m : (k + 1) * m] + moved[k].astype(F32) for k in range(self.size // 2)}
        if self.size == 8:
            half = m // 2
            last = have[6].astype(BF)
            four, two = self.swap(last[half:], 2), self.swap(last[:half], 4)
            mid4, mid2 = have[4].astype(BF), have[2].astype(BF)
            add4 = (have[4][half:] + four.astype(F32)).astype(BF)
            add2 = (have[2][:half] + two.astype(F32)).astype(BF)
            a = jnp.concatenate([self.swap(mid4[:half], 4), self.swap(add4, 4)], axis=0)
            b = jnp.concatenate([self.swap(add2, 2), self.swap(mid2[half:], 2)], axis=0)
            return have[0] + a.astype(F32) + b.astype(F32)
        for bit in self.bits[1:]:
            for k in [k for k in have if k & bit]:
                have[k ^ bit] = have[k ^ bit] + self.swap(have.pop(k).astype(BF), bit).astype(F32)
        return have[0]

    def sum_tokens(self, v):
        for bit in self.bits:
            v = v + self.swap_tokens(v, bit, 1)
        return v

    def sum_all(self, v):
        bit = 1
        while bit < self.count:
            v = v + self.swap(v, bit)
            bit *= 2
        return v


def per_device(layer_input, doc_lengths, w_qkv, w_out, w_gate_up, w_down, norm_gains, cotangent):
    c = Comm()
    copies, size, part = c.copies, c.size, c.part
    _, tl, d = layer_input.shape
    toks, row_len = tl * size, tl * c.seq
    heads = d // HD
    hl = heads // size
    wide = hl * HD
    n_in, n_out, n_ff = w_qkv.shape[0], w_out.shape[0], w_down.shape[0]
    ffl = n_ff * copies
    flat_in = layer_input.reshape(tl, d)
    pairs = 2 * n_out == HD and 2 * hl == copies
    half_group = size // 2

    if pairs:
        send_qkv = w_qkv.reshape(n_in, 3, 2, hl, half_group, HD).transpose(4, 2, 0, 1, 3, 5)
    else:
        send_qkv = w_qkv.reshape(n_in, 3, size, wide).transpose(2, 0, 1, 3)
    slab_qkv = c.exchange(send_qkv.reshape(size, n_in, 3 * wide)).reshape(size * n_in, 3 * wide)
    x_full = c.gather_tokens(flat_in)
    send_gu = w_gate_up.reshape(n_in, 2, copies, size, n_ff).transpose(3, 0, 1, 2, 4)
    send_gu = after(send_gu.reshape(size, n_in, 2 * ffl), slab_qkv)
    slab_gu = c.exchange(send_gu).reshape(size * n_in, 2 * ffl)

    full_out = c.gather(w_out)
    full_qkv = c.gather(slab_qkv)
    full_gu = c.gather(after(slab_gu, full_qkv))
    full_down = c.gather(after(w_down, full_qkv))

    lengths = doc_lengths.astype(jnp.int32)
    other = [lengths]
    for j in range(1, part):
        other.append(c.swap(lengths, j * c.seq))
    lengths = jnp.concatenate(other, axis=0)
    doc_ends = jnp.cumsum(lengths, axis=1)
    near = [k % c.seq for k in c.order if k < c.seq]
    places = jnp.concatenate([(c.s ^ k) * tl + jnp.arange(tl, dtype=jnp.int32) for k in near])
    passed = (places[None, :, None] >= doc_ends[:, None, :]).astype(jnp.int32)
    segment = jnp.sum(passed, axis=-1)
    positions = places[None, :] - jnp.sum(passed * lengths[:, None, :], axis=-1)
    allowed = (places[:, None] >= places[None, :])[None] & (segment[:, :, None] == segment[:, None, :])

    def by_rows(v):
        v = v.reshape((2, part, c.seq // 2, tl) + v.shape[1:])
        return v.swapaxes(0, 1).reshape((part, row_len) + v.shape[4:])

    def by_tokens(v):
        v = v.reshape((part, 2, c.seq // 2, tl) + v.shape[2:])
        return v.swapaxes(0, 1).reshape((toks,) + v.shape[4:])

    cosine, sine_table = rope_tables(by_tokens(positions))
    if pairs:
        gains4 = norm_gains.reshape(4, 2, hl, half_group, HD).transpose(3, 1, 0, 2, 4).reshape(size, 4, wide)
    else:
        gains4 = norm_gains.reshape(4, size, wide).transpose(1, 0, 2)
    gains_own = pick(gains4, c.g)

    mixed = dot_nn(x_full, full_qkv)
    query_pre, key_pre = mixed[:, :wide], mixed[:, wide : 2 * wide]
    squares = jnp.stack([jnp.sum(query_pre * query_pre, -1), jnp.sum(key_pre * key_pre, -1)])
    scales = lax.rsqrt(c.sum_tokens(squares) / d + eps)
    query_scale, key_scale = scales[0][:, None], scales[1][:, None]
    shape3 = (toks, hl, HD)
    query = rotate((query_pre * query_scale * gains_own[0]).reshape(shape3), cosine, sine_table, 1.0)
    key = rotate((key_pre * key_scale * gains_own[1]).reshape(shape3), cosine, sine_table, 1.0)
    query, key = by_rows(query.astype(BF)), by_rows(key.astype(BF))
    value = by_rows(mixed[:, 2 * wide :].reshape(shape3).astype(BF))
    score_scale = 1.0 / HD**0.5
    scores = jnp.einsum("rqhd,rkhd->rhqk", query, key, preferred_element_type=F32) * score_scale
    scores = jnp.where(allowed[:, None], scores, -1e30)
    row_max = jnp.max(scores, axis=-1, keepdims=True)
    exponent = jnp.exp(scores - row_max)
    probs = exponent / jnp.sum(exponent, axis=-1, keepdims=True)
    probs_low = probs.astype(BF)
    attended = jnp.einsum("rhqk,rkhd->rqhd", probs_low, value, preferred_element_type=F32).astype(BF)

    def to_out(v):
        if pairs:
            core = c.g % 2
            v = v.reshape(toks, hl, 2, HD // 2).transpose(2, 0, 1, 3).reshape(2, toks, wide // 2)
            own, got = pick(v, core), c.swap_tokens(pick(v, 1 - core), 1)
            first = jnp.where(core == 0, own, got)
            second = jnp.where(core == 0, got, own)
            return jnp.concatenate([first, second], axis=1)
        v = v.reshape(toks, wide // (size * n_out), size, n_out)
        v = c.exchange(v.transpose(2, 0, 1, 3).reshape(size, toks, wide // size), True)
        return v.transpose(1, 0, 2).reshape(toks, wide)

    def from_out(v):
        if pairs:
            core = c.g % 2
            v = v.reshape(toks, 2, wide // 2).transpose(1, 0, 2)
            own, got = pick(v, core), c.swap_tokens(pick(v, 1 - core), 1)
            first = jnp.where(core == 0, own, got).reshape(toks, hl, 1, HD // 2)
            second = jnp.where(core == 0, got, own).reshape(toks, hl, 1, HD // 2)
            return jnp.concatenate([first, second], axis=2).reshape(shape3)
        v = c.exchange(v.reshape(toks, size, wide // size).transpose(1, 0, 2), True)
        v = v.reshape(size, toks, wide // (size * n_out), n_out).transpose(1, 2, 0, 3)
        return v.reshape(shape3)

    attended = to_out(by_tokens(attended))
    branch = c.scatter_tokens(attended, lambda v: dot_nn(v, full_out))
    branch_scale = lax.rsqrt(jnp.mean(branch * branch, axis=-1, keepdims=True) + eps)
    hidden = flat_in.astype(F32) + branch * branch_scale * norm_gains[2]
    hidden_low = c.gather_tokens(hidden.astype(BF))

    gate_up = dot_nn(hidden_low, full_gu)
    gate, up = gate_up[:, :ffl], gate_up[:, ffl:]
    sig = jax.nn.sigmoid(gate)
    inner = (gate * sig * up).astype(BF)
    branch2 = c.scatter_tokens(inner, lambda v: dot_nn(v, full_down))
    branch2_scale = lax.rsqrt(jnp.mean(branch2 * branch2, axis=-1, keepdims=True) + eps)
    output = (hidden + branch2 * branch2_scale * norm_gains[3]).astype(BF)

    upstream = cotangent.reshape(tl, d).astype(F32)
    grad_branch2, gain_mlp = norm_back(branch2, branch2_scale, norm_gains[3], upstream)
    grad_branch2 = c.gather_tokens(grad_branch2.astype(BF))
    g_down = dot_tn(inner, grad_branch2).astype(BF)
    sum_down = c.scatter(g_down)
    grad_inner = dot_nt(grad_branch2, full_down)
    grad_gate = grad_inner * up * sig * (1.0 + gate * (1.0 - sig))
    grad_gu = jnp.concatenate([grad_gate, grad_inner * (gate * sig)], axis=1).astype(BF)
    g_gu = dot_tn(hidden_low, grad_gu).astype(BF)
    sum_gu = c.scatter(g_gu)
    grad_hidden = upstream + c.scatter_tokens(grad_gu, lambda v: dot_nt(v, full_gu))
    grad_branch, gain_attn = norm_back(branch, branch_scale, norm_gains[2], grad_hidden)
    grad_branch = c.gather_tokens(grad_branch.astype(BF))
    g_out = dot_tn(attended, grad_branch).astype(BF)
    sum_out = c.scatter(g_out)
    grad_att = by_rows(from_out(dot_nt(grad_branch, full_out).astype(BF)))
    grad_probs = jnp.einsum("rqhd,rkhd->rhqk", grad_att, value, preferred_element_type=F32)
    grad_value = jnp.einsum("rhqk,rqhd->rkhd", probs_low, grad_att, preferred_element_type=F32)
    row_sum = jnp.sum(probs * grad_probs, axis=-1, keepdims=True)
    grad_scores = (probs * (grad_probs - row_sum)).astype(BF)
    grad_query = jnp.einsum("rhqk,rkhd->rqhd", grad_scores, key, preferred_element_type=F32)
    grad_key = jnp.einsum("rhqk,rqhd->rkhd", grad_scores, query, preferred_element_type=F32)
    grad_query = by_tokens((grad_query * score_scale).astype(BF)).astype(F32)
    grad_key = by_tokens((grad_key * score_scale).astype(BF)).astype(F32)
    grad_value = by_tokens(grad_value.astype(BF)).reshape(toks, wide)
    e_query = rotate(grad_query, cosine, sine_table, -1.0).reshape(toks, wide)
    e_key = rotate(grad_key, cosine, sine_table, -1.0).reshape(toks, wide)
    scaled_q, scaled_k = e_query * gains_own[0], e_key * gains_own[1]
    means = c.sum_tokens(
        jnp.stack([jnp.sum(scaled_q * query_pre, -1), jnp.sum(scaled_k * key_pre, -1)])
    )
    means = means / d
    grad_qp = query_scale * scaled_q - query_pre * query_scale**3 * means[0][:, None]
    grad_kp = key_scale * scaled_k - key_pre * key_scale**3 * means[1][:, None]
    gain_query = jnp.sum(e_query * query_pre * query_scale, axis=0)
    gain_key = jnp.sum(e_key * key_pre * key_scale, axis=0)
    grad_mixed = jnp.concatenate([grad_qp.astype(BF), grad_kp.astype(BF), grad_value], axis=1)
    grad_mixed = after(grad_mixed, sum_down, sum_gu)
    g_qkv = dot_tn(x_full, grad_mixed).astype(BF)
    sum_qkv = c.scatter(g_qkv)
    grad_input = grad_hidden + c.scatter_tokens(grad_mixed, lambda v: dot_nt(v, full_qkv))

    back_gu = c.exchange(sum_gu.reshape(size, n_in, 2 * ffl)).astype(F32)
    back_gu = back_gu.reshape(size, n_in, 2, copies, n_ff)
    grad_gate_up = back_gu.transpose(1, 2, 3, 0, 4)
    back_qkv = c.exchange(sum_qkv.reshape(size, n_in, 3 * wide)).astype(F32)
    if pairs:
        grad_qkv = back_qkv.reshape(half_group, 2, n_in, 3, hl, HD).transpose(2, 3, 1, 4, 0, 5)
    else:
        grad_qkv = back_qkv.reshape(size, n_in, 3, wide).transpose(1, 2, 0, 3)

    own_terms = jnp.zeros((size, 2, wide), F32)
    own_terms = lax.dynamic_update_slice(own_terms, jnp.stack([gain_query, gain_key])[None], (c.g, 0, 0))
    if pairs:
        own_terms = own_terms.reshape(half_group, 2, 2, hl, HD).transpose(2, 1, 3, 0, 4)
    else:
        own_terms = own_terms.transpose(1, 0, 2)
    terms = jnp.concatenate([own_terms.reshape(2, d), jnp.stack([gain_attn, gain_mlp])])
    grad_gains = c.sum_all(terms)

    return (
        output.reshape(layer_input.shape),
        grad_input.reshape(layer_input.shape),
        grad_qkv.reshape(w_qkv.shape),
        sum_out.astype(F32),
        grad_gate_up.reshape(w_gate_up.shape),
        sum_down.astype(F32),
        grad_gains,
    )


def solution(mesh):
    both = P(("rows", "seq"), None)
    tokens = P("rows", "seq", None)
    return jax.shard_map(
        per_device,
        mesh=mesh,
        in_specs=(tokens, P("rows", None), both, both, both, both, P(), tokens),
        out_specs=(tokens, tokens, both, both, both, both, P()),
        check_vma=False,
    )
```

```python
import jax
import jax.numpy as jnp
from jax import lax
from jax.sharding import PartitionSpec as P

HD = 128
BF = jnp.bfloat16
F32 = jnp.float32

eps = 1e-06
rope_base = 500000.0


def rope_tables(positions):
    half_width = HD // 2
    frequency = jnp.power(rope_base, -(jnp.arange(half_width, dtype=F32) * 2.0) / HD)
    angles = positions.astype(F32)[:, None] * frequency
    cosine, sine_table = lax.optimization_barrier((jnp.cos(angles), jnp.sin(angles)))
    cosine = jnp.concatenate([cosine, cosine], axis=-1)
    sine_table = jnp.concatenate([sine_table, sine_table], axis=-1)
    return cosine[:, None, :], sine_table[:, None, :]


def rotate(tensor, cosine, sine_table, turn_sign):
    half_width = HD // 2
    turned = jnp.concatenate([-tensor[..., half_width:], tensor[..., :half_width]], axis=-1)
    return tensor * cosine + turn_sign * turned * sine_table


def dot_nn(a, b):
    return lax.dot_general(a, b, (((1,), (0,)), ((), ())), preferred_element_type=F32)


def dot_nt(a, b):
    return lax.dot_general(a, b, (((1,), (1,)), ((), ())), preferred_element_type=F32)


def dot_tn(a, b):
    return lax.dot_general(a, b, (((0,), (0,)), ((), ())), preferred_element_type=F32)


def pick(array, index):
    return lax.dynamic_index_in_dim(array, index, 0, keepdims=False)


def after(value, *others):
    return lax.optimization_barrier((value,) + others)[0]


def norm_back(tensor, inv_scale, gain_row, upstream):
    scaled = upstream * gain_row
    average = jnp.mean(scaled * tensor, axis=-1, keepdims=True)
    grad_tensor = inv_scale * scaled - tensor * (inv_scale * inv_scale * inv_scale) * average
    gain_term = jnp.sum(upstream * tensor * inv_scale, axis=0)
    return grad_tensor, gain_term


class Comm:
    def __init__(self, group=8):
        rows, seq = lax.axis_size("rows"), lax.axis_size("seq")
        self.part = max(1, min(rows, group // seq))
        self.copies, self.size, self.count = rows // self.part, self.part * seq, rows * seq
        row, s = lax.axis_index("rows"), lax.axis_index("seq")
        self.d = row // self.part
        self.g = (row % self.part) * seq + s
        self.seq, self.t, self.s = seq, row % self.part, s
        bits = [1 << i for i in range(self.size.bit_length() - 1)]
        self.bits = bits
        self.lines = [[i * self.size + g for i in range(self.copies)] for g in range(self.size)]
        self.order = list(range(0, self.size, 2)) + list(range(1, self.size, 2))

    def send(self, v, pairs):
        return lax.ppermute(v, ("rows", "seq"), pairs)

    def swap(self, v, j):
        return self.send(v, [(i, i ^ j) for i in range(self.count)])

    def gather(self, block):
        return lax.all_gather(block, ("rows", "seq"), axis=0, tiled=True, axis_index_groups=self.lines)

    def scatter(self, parts):
        return lax.psum_scatter(
            parts, ("rows", "seq"), scatter_dimension=0, tiled=True, axis_index_groups=self.lines
        )

    def exchange(self, parts, tokens=False):
        shape = parts.shape
        swap = self.swap if not tokens else lambda v, j: self.swap_tokens(v, j, 1)
        parts = parts.reshape((self.size // 2, 2) + shape[1:])
        core, pair = self.g % 2, self.g // 2
        other = swap(lax.dynamic_index_in_dim(parts, 1 - core, 1, keepdims=False), 1)
        parts = lax.dynamic_update_index_in_dim(parts, other, 1 - core, 1)
        moved = [swap(pick(parts, pair ^ j), 2 * j) for j in range(1, self.size // 2)]
        for j, v in enumerate(moved):
            parts = lax.dynamic_update_index_in_dim(parts, v, pair ^ (j + 1), 0)
        return parts.reshape(shape)

    def swap_tokens(self, v, j, axis=0):
        pieces = jnp.split(self.swap(v, j), self.size, axis=axis)
        place = {k: p for p, k in enumerate(self.order)}
        return jnp.concatenate([pieces[place[k ^ j]] for k in self.order], axis=axis)

    def gather_tokens(self, v):
        got = {0: v}
        if self.size == 8:
            half = v.shape[0] // 2
            got[4], got[2] = self.swap(v, 4), self.swap(v, 2)
            got[1] = self.swap(v, 1)
            got[6] = jnp.concatenate([self.swap(got[4][:half], 2), self.swap(got[2][half:], 4)], axis=0)
            for k in (2, 4, 6):
                got[k + 1] = self.swap(got[k], 1)
        else:
            for bit in self.bits[::-1]:
                for k in sorted(got):
                    got[k | bit] = self.swap(got[k], bit)
        return jnp.concatenate([got[k] for k in self.order], axis=0)

    def scatter_tokens(self, tokens, make_dot):
        n = tokens.shape[0] // 2
        away = make_dot(tokens[n:]).astype(BF)
        m = n // (self.size // 2)
        moved = [self.swap(away[k * m : (k + 1) * m], 1) for k in range(self.size // 2)]
        kept = make_dot(tokens[:n])
        have = {2 * k: kept[k * m : (k + 1) * m] + moved[k].astype(F32) for k in range(self.size // 2)}
        if self.size == 8:
            half = m // 2
            last = have[6].astype(BF)
            four, two = self.swap(last[half:], 2), self.swap(last[:half], 4)
            mid4, mid2 = have[4].astype(BF), have[2].astype(BF)
            add4 = (have[4][half:] + four.astype(F32)).astype(BF)
            add2 = (have[2][:half] + two.astype(F32)).astype(BF)
            a = jnp.concatenate([self.swap(mid4[:half], 4), self.swap(add4, 4)], axis=0)
            b = jnp.concatenate([self.swap(add2, 2), self.swap(mid2[half:], 2)], axis=0)
            return have[0] + a.astype(F32) + b.astype(F32)
        for bit in self.bits[1:]:
            for k in [k for k in have if k & bit]:
                have[k ^ bit] = have[k ^ bit] + self.swap(have.pop(k).astype(BF), bit).astype(F32)
        return have[0]

    def sum_tokens(self, v):
        for bit in self.bits:
            v = v + self.swap_tokens(v, bit, 1)
        return v

    def sum_all(self, v):
        bit = 1
        while bit < self.count:
            v = v + self.swap(v, bit)
            bit *= 2
        return v


def per_device(layer_input, doc_lengths, w_qkv, w_out, w_gate_up, w_down, norm_gains, cotangent):
    c = Comm()
    copies, size, part = c.copies, c.size, c.part
    _, tl, d = layer_input.shape
    toks, row_len = tl * size, tl * c.seq
    heads = d // HD
    hl = heads // size
    wide = hl * HD
    n_in, n_out, n_ff = w_qkv.shape[0], w_out.shape[0], w_down.shape[0]
    ffl = n_ff * copies
    flat_in = layer_input.reshape(tl, d)
    pairs = 2 * n_out == HD and 2 * hl == copies
    half_group = size // 2

    lengths = doc_lengths.astype(jnp.int32)
    lengths = [lengths] + [c.swap(lengths, j * c.seq) for j in range(1, part)]
    lengths = jnp.concatenate(lengths, axis=0)

    full_out = c.gather(w_out)
    if pairs:
        send_qkv = w_qkv.reshape(n_in, 3, 2, hl, half_group, HD).transpose(4, 2, 0, 1, 3, 5)
    else:
        send_qkv = w_qkv.reshape(n_in, 3, size, wide).transpose(2, 0, 1, 3)
    slab_qkv = c.exchange(send_qkv.reshape(size, n_in, 3 * wide)).reshape(size * n_in, 3 * wide)
    full_qkv = c.gather(after(slab_qkv, full_out))
    x_full = c.gather_tokens(after(flat_in, lengths))
    send_gu = w_gate_up.reshape(n_in, 2, copies, size, n_ff).transpose(3, 0, 1, 2, 4)
    send_gu = after(send_gu.reshape(size, n_in, 2 * ffl), x_full)
    slab_gu = c.exchange(send_gu).reshape(size * n_in, 2 * ffl)
    full_gu = c.gather(after(slab_gu, full_qkv))
    full_down = c.gather(after(w_down, full_qkv))

    lengths = after(lengths, x_full)
    doc_ends = jnp.cumsum(lengths, axis=1)
    near = [k % c.seq for k in c.order if k < c.seq]
    places = jnp.concatenate([(c.s ^ k) * tl + jnp.arange(tl, dtype=jnp.int32) for k in near])
    passed = (places[None, :, None] >= doc_ends[:, None, :]).astype(jnp.int32)
    segment = jnp.sum(passed, axis=-1)
    positions = places[None, :] - jnp.sum(passed * lengths[:, None, :], axis=-1)
    allowed = (places[:, None] >= places[None, :])[None] & (segment[:, :, None] == segment[:, None, :])

    def by_rows(v):
        v = v.reshape((2, part, c.seq // 2, tl) + v.shape[1:])
        return v.swapaxes(0, 1).reshape((part, row_len) + v.shape[4:])

    def by_tokens(v):
        v = v.reshape((part, 2, c.seq // 2, tl) + v.shape[2:])
        return v.swapaxes(0, 1).reshape((toks,) + v.shape[4:])

    cosine, sine_table = rope_tables(by_tokens(positions))
    if pairs:
        gains4 = norm_gains.reshape(4, 2, hl, half_group, HD).transpose(3, 1, 0, 2, 4).reshape(size, 4, wide)
    else:
        gains4 = norm_gains.reshape(4, size, wide).transpose(1, 0, 2)
    gains_own = pick(gains4, c.g)

    mixed = dot_nn(after(x_full, slab_gu), full_qkv)
    query_pre, key_pre = mixed[:, :wide], mixed[:, wide : 2 * wide]
    squares = jnp.stack([jnp.sum(query_pre * query_pre, -1), jnp.sum(key_pre * key_pre, -1)])
    scales = lax.rsqrt(c.sum_tokens(squares) / d + eps)
    query_scale, key_scale = scales[0][:, None], scales[1][:, None]
    shape3 = (toks, hl, HD)
    query = rotate((query_pre * query_scale * gains_own[0]).reshape(shape3), cosine, sine_table, 1.0)
    key = rotate((key_pre * key_scale * gains_own[1]).reshape(shape3), cosine, sine_table, 1.0)
    query, key = by_rows(query.astype(BF)), by_rows(key.astype(BF))
    value = by_rows(mixed[:, 2 * wide :].reshape(shape3).astype(BF))
    score_scale = 1.0 / HD**0.5
    scores = jnp.einsum("rqhd,rkhd->rhqk", query, key, preferred_element_type=F32) * score_scale
    scores = jnp.where(allowed[:, None], scores, -1e30)
    row_max = jnp.max(scores, axis=-1, keepdims=True)
    exponent = jnp.exp(scores - row_max)
    probs = exponent / jnp.sum(exponent, axis=-1, keepdims=True)
    probs_low = probs.astype(BF)
    attended = jnp.einsum("rhqk,rkhd->rqhd", probs_low, value, preferred_element_type=F32).astype(BF)

    def to_out(v):
        if pairs:
            core = c.g % 2
            v = v.reshape(toks, hl, 2, HD // 2).transpose(2, 0, 1, 3).reshape(2, toks, wide // 2)
            own, got = pick(v, core), c.swap_tokens(pick(v, 1 - core), 1)
            first = jnp.where(core == 0, own, got)
            second = jnp.where(core == 0, got, own)
            return jnp.concatenate([first, second], axis=1)
        v = v.reshape(toks, wide // (size * n_out), size, n_out)
        v = c.exchange(v.transpose(2, 0, 1, 3).reshape(size, toks, wide // size), True)
        return v.transpose(1, 0, 2).reshape(toks, wide)

    def from_out(v):
        if pairs:
            core = c.g % 2
            v = v.reshape(toks, 2, wide // 2).transpose(1, 0, 2)
            own, got = pick(v, core), c.swap_tokens(pick(v, 1 - core), 1)
            first = jnp.where(core == 0, own, got).reshape(toks, hl, 1, HD // 2)
            second = jnp.where(core == 0, got, own).reshape(toks, hl, 1, HD // 2)
            return jnp.concatenate([first, second], axis=2).reshape(shape3)
        v = c.exchange(v.reshape(toks, size, wide // size).transpose(1, 0, 2), True)
        v = v.reshape(size, toks, wide // (size * n_out), n_out).transpose(1, 2, 0, 3)
        return v.reshape(shape3)

    attended = to_out(by_tokens(attended))
    branch = c.scatter_tokens(attended, lambda v: dot_nn(v, full_out))
    branch_scale = lax.rsqrt(jnp.mean(branch * branch, axis=-1, keepdims=True) + eps)
    hidden = flat_in.astype(F32) + branch * branch_scale * norm_gains[2]
    hidden_low = c.gather_tokens(hidden.astype(BF))

    gate_up = dot_nn(hidden_low, full_gu)
    gate, up = gate_up[:, :ffl], gate_up[:, ffl:]
    sig = jax.nn.sigmoid(gate)
    inner = (gate * sig * up).astype(BF)
    branch2 = c.scatter_tokens(inner, lambda v: dot_nn(v, full_down))
    branch2_scale = lax.rsqrt(jnp.mean(branch2 * branch2, axis=-1, keepdims=True) + eps)
    output = (hidden + branch2 * branch2_scale * norm_gains[3]).astype(BF)

    upstream = cotangent.reshape(tl, d).astype(F32)
    grad_branch2, gain_mlp = norm_back(branch2, branch2_scale, norm_gains[3], upstream)
    grad_branch2 = c.gather_tokens(grad_branch2.astype(BF))
    g_down = dot_tn(inner, grad_branch2).astype(BF)
    sum_down = c.scatter(g_down)
    grad_inner = dot_nt(grad_branch2, full_down)
    grad_gate = grad_inner * up * sig * (1.0 + gate * (1.0 - sig))
    grad_gu = jnp.concatenate([grad_gate, grad_inner * (gate * sig)], axis=1).astype(BF)
    g_gu = dot_tn(hidden_low, grad_gu).astype(BF)
    sum_gu = c.scatter(g_gu)
    grad_hidden = upstream + c.scatter_tokens(grad_gu, lambda v: dot_nt(v, full_gu))
    grad_branch, gain_attn = norm_back(branch, branch_scale, norm_gains[2], grad_hidden)
    grad_branch = c.gather_tokens(grad_branch.astype(BF))
    g_out = dot_tn(attended, grad_branch).astype(BF)
    sum_out = c.scatter(g_out)
    grad_att = by_rows(from_out(dot_nt(grad_branch, full_out).astype(BF)))
    grad_probs = jnp.einsum("rqhd,rkhd->rhqk", grad_att, value, preferred_element_type=F32)
    grad_value = jnp.einsum("rhqk,rqhd->rkhd", probs_low, grad_att, preferred_element_type=F32)
    row_sum = jnp.sum(probs * grad_probs, axis=-1, keepdims=True)
    grad_scores = (probs * (grad_probs - row_sum)).astype(BF)
    grad_query = jnp.einsum("rhqk,rkhd->rqhd", grad_scores, key, preferred_element_type=F32)
    grad_key = jnp.einsum("rhqk,rqhd->rkhd", grad_scores, query, preferred_element_type=F32)
    grad_query = by_tokens((grad_query * score_scale).astype(BF)).astype(F32)
    grad_key = by_tokens((grad_key * score_scale).astype(BF)).astype(F32)
    grad_value = by_tokens(grad_value.astype(BF)).reshape(toks, wide)
    e_query = rotate(grad_query, cosine, sine_table, -1.0).reshape(toks, wide)
    e_key = rotate(grad_key, cosine, sine_table, -1.0).reshape(toks, wide)
    scaled_q, scaled_k = e_query * gains_own[0], e_key * gains_own[1]
    means = c.sum_tokens(
        jnp.stack([jnp.sum(scaled_q * query_pre, -1), jnp.sum(scaled_k * key_pre, -1)])
    )
    means = means / d
    grad_qp = query_scale * scaled_q - query_pre * query_scale**3 * means[0][:, None]
    grad_kp = key_scale * scaled_k - key_pre * key_scale**3 * means[1][:, None]
    gain_query = jnp.sum(e_query * query_pre * query_scale, axis=0)
    gain_key = jnp.sum(e_key * key_pre * key_scale, axis=0)
    grad_mixed = jnp.concatenate([grad_qp.astype(BF), grad_kp.astype(BF), grad_value], axis=1)
    grad_mixed = after(grad_mixed, sum_down, sum_gu)
    g_qkv = dot_tn(x_full, grad_mixed).astype(BF)
    sum_qkv = c.scatter(g_qkv)
    back_gu = c.exchange(sum_gu.reshape(size, n_in, 2 * ffl)).astype(F32)
    back_gu = back_gu.reshape(size, n_in, 2, copies, n_ff)
    grad_gate_up = back_gu.transpose(1, 2, 3, 0, 4)
    grad_mixed = after(grad_mixed, g_qkv, back_gu)
    grad_input = grad_hidden + c.scatter_tokens(grad_mixed, lambda v: dot_nt(v, full_qkv))

    back_qkv = c.exchange(sum_qkv.reshape(size, n_in, 3 * wide)).astype(F32)
    if pairs:
        grad_qkv = back_qkv.reshape(half_group, 2, n_in, 3, hl, HD).transpose(2, 3, 1, 4, 0, 5)
    else:
        grad_qkv = back_qkv.reshape(size, n_in, 3, wide).transpose(1, 2, 0, 3)

    own_terms = jnp.zeros((size, 2, wide), F32)
    own_terms = lax.dynamic_update_slice(own_terms, jnp.stack([gain_query, gain_key])[None], (c.g, 0, 0))
    if pairs:
        own_terms = own_terms.reshape(half_group, 2, 2, hl, HD).transpose(2, 1, 3, 0, 4)
    else:
        own_terms = own_terms.transpose(1, 0, 2)
    terms = jnp.concatenate([own_terms.reshape(2, d), jnp.stack([gain_attn, gain_mlp])])
    grad_gains = c.sum_all(terms)

    return (
        output.reshape(layer_input.shape),
        grad_input.reshape(layer_input.shape),
        grad_qkv.reshape(w_qkv.shape),
        sum_out.astype(F32),
        grad_gate_up.reshape(w_gate_up.shape),
        sum_down.astype(F32),
        grad_gains,
    )


def solution(mesh):
    both = P(("rows", "seq"), None)
    tokens = P("rows", "seq", None)
    return jax.shard_map(
        per_device,
        mesh=mesh,
        in_specs=(tokens, P("rows", None), both, both, both, both, P(), tokens),
        out_specs=(tokens, tokens, both, both, both, both, P()),
        check_vma=False,
    )
```

```python
import jax
import jax.numpy as jnp
from jax import lax
from jax.sharding import PartitionSpec as P

HD = 128
BF = jnp.bfloat16
F32 = jnp.float32

eps = 1e-06
rope_base = 500000.0


def rope_tables(positions):
    half_width = HD // 2
    frequency = jnp.power(rope_base, -(jnp.arange(half_width, dtype=F32) * 2.0) / HD)
    angles = positions.astype(F32)[:, None] * frequency
    cosine, sine_table = lax.optimization_barrier((jnp.cos(angles), jnp.sin(angles)))
    cosine = jnp.concatenate([cosine, cosine], axis=-1)
    sine_table = jnp.concatenate([sine_table, sine_table], axis=-1)
    return cosine[:, None, :], sine_table[:, None, :]


def rotate(tensor, cosine, sine_table, turn_sign):
    half_width = HD // 2
    turned = jnp.concatenate([-tensor[..., half_width:], tensor[..., :half_width]], axis=-1)
    return tensor * cosine + turn_sign * turned * sine_table


def dot_nn(a, b):
    return lax.dot_general(a, b, (((1,), (0,)), ((), ())), preferred_element_type=F32)


def dot_nt(a, b):
    return lax.dot_general(a, b, (((1,), (1,)), ((), ())), preferred_element_type=F32)


def dot_tn(a, b):
    return lax.dot_general(a, b, (((0,), (0,)), ((), ())), preferred_element_type=F32)


def pick(array, index):
    return lax.dynamic_index_in_dim(array, index, 0, keepdims=False)


def after(value, *others):
    return lax.optimization_barrier((value,) + others)[0]


def norm_back(tensor, inv_scale, gain_row, upstream):
    scaled = upstream * gain_row
    average = jnp.mean(scaled * tensor, axis=-1, keepdims=True)
    grad_tensor = inv_scale * scaled - tensor * (inv_scale * inv_scale * inv_scale) * average
    gain_term = jnp.sum(upstream * tensor * inv_scale, axis=0)
    return grad_tensor, gain_term


class Comm:
    def __init__(self, group=8):
        rows, seq = lax.axis_size("rows"), lax.axis_size("seq")
        self.part = max(1, min(rows, group // seq))
        self.copies, self.size, self.count = rows // self.part, self.part * seq, rows * seq
        row, s = lax.axis_index("rows"), lax.axis_index("seq")
        self.d = row // self.part
        self.g = (row % self.part) * seq + s
        self.seq, self.t, self.s = seq, row % self.part, s
        bits = [1 << i for i in range(self.size.bit_length() - 1)]
        self.bits = bits
        self.lines = [[i * self.size + g for i in range(self.copies)] for g in range(self.size)]
        self.order = list(range(0, self.size, 2)) + list(range(1, self.size, 2))

    def send(self, v, pairs):
        return lax.ppermute(v, ("rows", "seq"), pairs)

    def swap(self, v, j):
        return self.send(v, [(i, i ^ j) for i in range(self.count)])

    def gather(self, block):
        return lax.all_gather(block, ("rows", "seq"), axis=0, tiled=True, axis_index_groups=self.lines)

    def scatter(self, parts):
        return lax.psum_scatter(
            parts, ("rows", "seq"), scatter_dimension=0, tiled=True, axis_index_groups=self.lines
        )

    def exchange(self, parts, tokens=False):
        shape = parts.shape
        swap = self.swap if not tokens else lambda v, j: self.swap_tokens(v, j, 1)
        parts = parts.reshape((self.size // 2, 2) + shape[1:])
        core, pair = self.g % 2, self.g // 2
        other = swap(lax.dynamic_index_in_dim(parts, 1 - core, 1, keepdims=False), 1)
        parts = lax.dynamic_update_index_in_dim(parts, other, 1 - core, 1)
        moved = [swap(pick(parts, pair ^ j), 2 * j) for j in range(1, self.size // 2)]
        for j, v in enumerate(moved):
            parts = lax.dynamic_update_index_in_dim(parts, v, pair ^ (j + 1), 0)
        return parts.reshape(shape)

    def swap_tokens(self, v, j, axis=0):
        pieces = jnp.split(self.swap(v, j), self.size, axis=axis)
        place = {k: p for p, k in enumerate(self.order)}
        return jnp.concatenate([pieces[place[k ^ j]] for k in self.order], axis=axis)

    def gather_tokens(self, v):
        got = {0: v}
        if self.size == 8:
            half = v.shape[0] // 2
            got[4], got[2] = self.swap(v, 4), self.swap(v, 2)
            got[1] = self.swap(v, 1)
            got[6] = jnp.concatenate([self.swap(got[4][:half], 2), self.swap(got[2][half:], 4)], axis=0)
            for k in (2, 4, 6):
                got[k + 1] = self.swap(got[k], 1)
        else:
            for bit in self.bits[::-1]:
                for k in sorted(got):
                    got[k | bit] = self.swap(got[k], bit)
        return jnp.concatenate([got[k] for k in self.order], axis=0)

    def scatter_tokens(self, tokens, make_dot):
        n = tokens.shape[0] // 2
        away = make_dot(tokens[n:]).astype(BF)
        m = n // (self.size // 2)
        moved = [self.swap(away[k * m : (k + 1) * m], 1) for k in range(self.size // 2)]
        kept = make_dot(tokens[:n])
        have = {2 * k: kept[k * m : (k + 1) * m] + moved[k].astype(F32) for k in range(self.size // 2)}
        if self.size == 8:
            half = m // 2
            last = have[6].astype(BF)
            four, two = self.swap(last[half:], 2), self.swap(last[:half], 4)
            mid4, mid2 = have[4].astype(BF), have[2].astype(BF)
            add4 = (have[4][half:] + four.astype(F32)).astype(BF)
            add2 = (have[2][:half] + two.astype(F32)).astype(BF)
            a = jnp.concatenate([self.swap(mid4[:half], 4), self.swap(add4, 4)], axis=0)
            b = jnp.concatenate([self.swap(add2, 2), self.swap(mid2[half:], 2)], axis=0)
            return have[0] + a.astype(F32) + b.astype(F32)
        for bit in self.bits[1:]:
            for k in [k for k in have if k & bit]:
                have[k ^ bit] = have[k ^ bit] + self.swap(have.pop(k).astype(BF), bit).astype(F32)
        return have[0]

    def sum_tokens(self, v):
        for bit in self.bits:
            v = v + self.swap_tokens(v, bit, 1)
        return v

    def sum_all(self, v):
        bit = 1
        while bit < self.count:
            v = v + self.swap(v, bit)
            bit *= 2
        return v


def per_device(layer_input, doc_lengths, w_qkv, w_out, w_gate_up, w_down, norm_gains, cotangent):
    c = Comm()
    copies, size, part = c.copies, c.size, c.part
    _, tl, d = layer_input.shape
    toks, row_len = tl * size, tl * c.seq
    heads = d // HD
    hl = heads // size
    wide = hl * HD
    n_in, n_out, n_ff = w_qkv.shape[0], w_out.shape[0], w_down.shape[0]
    ffl = n_ff * copies
    flat_in = layer_input.reshape(tl, d)
    pairs = 2 * n_out == HD and 2 * hl == copies
    half_group = size // 2

    lengths = doc_lengths.astype(jnp.int32)
    lengths = [lengths] + [c.swap(lengths, j * c.seq) for j in range(1, part)]
    lengths = jnp.concatenate(lengths, axis=0)

    if pairs:
        send_qkv = w_qkv.reshape(n_in, 3, 2, hl, half_group, HD).transpose(4, 2, 0, 1, 3, 5)
    else:
        send_qkv = w_qkv.reshape(n_in, 3, size, wide).transpose(2, 0, 1, 3)
    slab_qkv = c.exchange(send_qkv.reshape(size, n_in, 3 * wide)).reshape(size * n_in, 3 * wide)
    full_qkv = c.gather(slab_qkv)
    full_out = c.gather(w_out)
    x_full = c.gather_tokens(after(flat_in, slab_qkv, lengths))
    send_gu = w_gate_up.reshape(n_in, 2, copies, size, n_ff).transpose(3, 0, 1, 2, 4)
    send_gu = after(send_gu.reshape(size, n_in, 2 * ffl), x_full)
    slab_gu = c.exchange(send_gu).reshape(size * n_in, 2 * ffl)
    x_full, slab_gu = lax.optimization_barrier((x_full, slab_gu))
    full_gu = c.gather(slab_gu)
    full_down = c.gather(after(w_down, full_qkv))

    lengths = after(lengths, x_full)
    doc_ends = jnp.cumsum(lengths, axis=1)
    near = [k % c.seq for k in c.order if k < c.seq]
    places = jnp.concatenate([(c.s ^ k) * tl + jnp.arange(tl, dtype=jnp.int32) for k in near])
    passed = (places[None, :, None] >= doc_ends[:, None, :]).astype(jnp.int32)
    segment = jnp.sum(passed, axis=-1)
    positions = places[None, :] - jnp.sum(passed * lengths[:, None, :], axis=-1)
    allowed = (places[:, None] >= places[None, :])[None] & (segment[:, :, None] == segment[:, None, :])

    def by_rows(v):
        v = v.reshape((2, part, c.seq // 2, tl) + v.shape[1:])
        return v.swapaxes(0, 1).reshape((part, row_len) + v.shape[4:])

    def by_tokens(v):
        v = v.reshape((part, 2, c.seq // 2, tl) + v.shape[2:])
        return v.swapaxes(0, 1).reshape((toks,) + v.shape[4:])

    cosine, sine_table = rope_tables(by_tokens(positions))
    if pairs:
        gains4 = norm_gains.reshape(4, 2, hl, half_group, HD).transpose(3, 1, 0, 2, 4).reshape(size, 4, wide)
    else:
        gains4 = norm_gains.reshape(4, size, wide).transpose(1, 0, 2)
    gains_own = pick(gains4, c.g)

    mixed = dot_nn(x_full, full_qkv)
    query_pre, key_pre = mixed[:, :wide], mixed[:, wide : 2 * wide]
    squares = jnp.stack([jnp.sum(query_pre * query_pre, -1), jnp.sum(key_pre * key_pre, -1)])
    scales = lax.rsqrt(c.sum_tokens(squares) / d + eps)
    query_scale, key_scale = scales[0][:, None], scales[1][:, None]
    shape3 = (toks, hl, HD)
    query = rotate((query_pre * query_scale * gains_own[0]).reshape(shape3), cosine, sine_table, 1.0)
    key = rotate((key_pre * key_scale * gains_own[1]).reshape(shape3), cosine, sine_table, 1.0)
    query, key = by_rows(query.astype(BF)), by_rows(key.astype(BF))
    value = by_rows(mixed[:, 2 * wide :].reshape(shape3).astype(BF))
    score_scale = 1.0 / HD**0.5
    scores = jnp.einsum("rqhd,rkhd->rhqk", query, key, preferred_element_type=F32) * score_scale
    scores = jnp.where(allowed[:, None], scores, -1e30)
    row_max = jnp.max(scores, axis=-1, keepdims=True)
    exponent = jnp.exp(scores - row_max)
    probs = exponent / jnp.sum(exponent, axis=-1, keepdims=True)
    probs_low = probs.astype(BF)
    attended = jnp.einsum("rhqk,rkhd->rqhd", probs_low, value, preferred_element_type=F32).astype(BF)

    def to_out(v):
        if pairs:
            core = c.g % 2
            v = v.reshape(toks, hl, 2, HD // 2).transpose(2, 0, 1, 3).reshape(2, toks, wide // 2)
            own, got = pick(v, core), c.swap_tokens(pick(v, 1 - core), 1)
            first = jnp.where(core == 0, own, got)
            second = jnp.where(core == 0, got, own)
            return jnp.concatenate([first, second], axis=1)
        v = v.reshape(toks, wide // (size * n_out), size, n_out)
        v = c.exchange(v.transpose(2, 0, 1, 3).reshape(size, toks, wide // size), True)
        return v.transpose(1, 0, 2).reshape(toks, wide)

    def from_out(v):
        if pairs:
            core = c.g % 2
            v = v.reshape(toks, 2, wide // 2).transpose(1, 0, 2)
            own, got = pick(v, core), c.swap_tokens(pick(v, 1 - core), 1)
            first = jnp.where(core == 0, own, got).reshape(toks, hl, 1, HD // 2)
            second = jnp.where(core == 0, got, own).reshape(toks, hl, 1, HD // 2)
            return jnp.concatenate([first, second], axis=2).reshape(shape3)
        v = c.exchange(v.reshape(toks, size, wide // size).transpose(1, 0, 2), True)
        v = v.reshape(size, toks, wide // (size * n_out), n_out).transpose(1, 2, 0, 3)
        return v.reshape(shape3)

    attended = to_out(by_tokens(attended))
    branch = c.scatter_tokens(attended, lambda v: dot_nn(v, full_out))
    branch_scale = lax.rsqrt(jnp.mean(branch * branch, axis=-1, keepdims=True) + eps)
    hidden = flat_in.astype(F32) + branch * branch_scale * norm_gains[2]
    hidden_low = c.gather_tokens(hidden.astype(BF))

    gate_up = dot_nn(hidden_low, full_gu)
    gate, up = gate_up[:, :ffl], gate_up[:, ffl:]
    sig = jax.nn.sigmoid(gate)
    inner = (gate * sig * up).astype(BF)
    branch2 = c.scatter_tokens(inner, lambda v: dot_nn(v, full_down))
    branch2_scale = lax.rsqrt(jnp.mean(branch2 * branch2, axis=-1, keepdims=True) + eps)
    output = (hidden + branch2 * branch2_scale * norm_gains[3]).astype(BF)

    upstream = cotangent.reshape(tl, d).astype(F32)
    grad_branch2, gain_mlp = norm_back(branch2, branch2_scale, norm_gains[3], upstream)
    grad_branch2 = c.gather_tokens(grad_branch2.astype(BF))
    g_down = dot_tn(inner, grad_branch2).astype(BF)
    sum_down = c.scatter(g_down)
    grad_inner = dot_nt(grad_branch2, full_down)
    grad_gate = grad_inner * up * sig * (1.0 + gate * (1.0 - sig))
    grad_gu = jnp.concatenate([grad_gate, grad_inner * (gate * sig)], axis=1).astype(BF)
    grad_hidden = upstream + c.scatter_tokens(grad_gu, lambda v: dot_nt(v, full_gu))
    g_gu = dot_tn(hidden_low, grad_gu).astype(BF)
    sum_gu = c.scatter(g_gu)
    grad_branch, gain_attn = norm_back(branch, branch_scale, norm_gains[2], grad_hidden)
    grad_branch = c.gather_tokens(grad_branch.astype(BF))
    grad_branch = after(grad_branch, sum_down)
    g_out = dot_tn(attended, grad_branch).astype(BF)
    sum_out = c.scatter(g_out)
    grad_att = by_rows(from_out(dot_nt(grad_branch, full_out).astype(BF)))
    grad_probs = jnp.einsum("rqhd,rkhd->rhqk", grad_att, value, preferred_element_type=F32)
    grad_value = jnp.einsum("rhqk,rqhd->rkhd", probs_low, grad_att, preferred_element_type=F32)
    row_sum = jnp.sum(probs * grad_probs, axis=-1, keepdims=True)
    grad_scores = (probs * (grad_probs - row_sum)).astype(BF)
    grad_query = jnp.einsum("rhqk,rkhd->rqhd", grad_scores, key, preferred_element_type=F32)
    grad_key = jnp.einsum("rhqk,rqhd->rkhd", grad_scores, query, preferred_element_type=F32)
    grad_query = by_tokens((grad_query * score_scale).astype(BF)).astype(F32)
    grad_key = by_tokens((grad_key * score_scale).astype(BF)).astype(F32)
    grad_value = by_tokens(grad_value.astype(BF)).reshape(toks, wide)
    e_query = rotate(grad_query, cosine, sine_table, -1.0).reshape(toks, wide)
    e_key = rotate(grad_key, cosine, sine_table, -1.0).reshape(toks, wide)
    scaled_q, scaled_k = e_query * gains_own[0], e_key * gains_own[1]
    means = c.sum_tokens(
        jnp.stack([jnp.sum(scaled_q * query_pre, -1), jnp.sum(scaled_k * key_pre, -1)])
    )
    means = means / d
    grad_qp = query_scale * scaled_q - query_pre * query_scale**3 * means[0][:, None]
    grad_kp = key_scale * scaled_k - key_pre * key_scale**3 * means[1][:, None]
    gain_query = jnp.sum(e_query * query_pre * query_scale, axis=0)
    gain_key = jnp.sum(e_key * key_pre * key_scale, axis=0)
    grad_mixed = jnp.concatenate([grad_qp.astype(BF), grad_kp.astype(BF), grad_value], axis=1)
    grad_mixed = after(grad_mixed, sum_down, sum_gu)
    g_qkv = dot_tn(x_full, grad_mixed).astype(BF)
    sum_qkv = c.scatter(g_qkv)
    grad_input = grad_hidden + c.scatter_tokens(grad_mixed, lambda v: dot_nt(v, full_qkv))

    back_gu = c.exchange(sum_gu.reshape(size, n_in, 2 * ffl)).astype(F32)
    back_gu = back_gu.reshape(size, n_in, 2, copies, n_ff)
    grad_gate_up = back_gu.transpose(1, 2, 3, 0, 4)
    back_qkv = c.exchange(sum_qkv.reshape(size, n_in, 3 * wide)).astype(F32)
    if pairs:
        grad_qkv = back_qkv.reshape(half_group, 2, n_in, 3, hl, HD).transpose(2, 3, 1, 4, 0, 5)
    else:
        grad_qkv = back_qkv.reshape(size, n_in, 3, wide).transpose(1, 2, 0, 3)

    own_terms = jnp.zeros((size, 2, wide), F32)
    own_terms = lax.dynamic_update_slice(own_terms, jnp.stack([gain_query, gain_key])[None], (c.g, 0, 0))
    if pairs:
        own_terms = own_terms.reshape(half_group, 2, 2, hl, HD).transpose(2, 1, 3, 0, 4)
    else:
        own_terms = own_terms.transpose(1, 0, 2)
    terms = jnp.concatenate([own_terms.reshape(2, d), jnp.stack([gain_attn, gain_mlp])])
    grad_gains = c.sum_all(terms)

    return (
        output.reshape(layer_input.shape),
        grad_input.reshape(layer_input.shape),
        grad_qkv.reshape(w_qkv.shape),
        sum_out.astype(F32),
        grad_gate_up.reshape(w_gate_up.shape),
        sum_down.astype(F32),
        grad_gains,
    )


def solution(mesh):
    both = P(("rows", "seq"), None)
    tokens = P("rows", "seq", None)
    return jax.shard_map(
        per_device,
        mesh=mesh,
        in_specs=(tokens, P("rows", None), both, both, both, both, P(), tokens),
        out_specs=(tokens, tokens, both, both, both, both, P()),
        check_vma=False,
    )
```

```python
import jax
import jax.numpy as jnp
from jax import lax
from jax.sharding import PartitionSpec as P

HD = 128
BF = jnp.bfloat16
F32 = jnp.float32

eps = 1e-06
rope_base = 500000.0


def rope_tables(positions):
    half_width = HD // 2
    frequency = jnp.power(rope_base, -(jnp.arange(half_width, dtype=F32) * 2.0) / HD)
    angles = positions.astype(F32)[:, None] * frequency
    cosine, sine_table = lax.optimization_barrier((jnp.cos(angles), jnp.sin(angles)))
    cosine = jnp.concatenate([cosine, cosine], axis=-1)
    sine_table = jnp.concatenate([sine_table, sine_table], axis=-1)
    return cosine[:, None, :], sine_table[:, None, :]


def rotate(tensor, cosine, sine_table, turn_sign):
    half_width = HD // 2
    turned = jnp.concatenate([-tensor[..., half_width:], tensor[..., :half_width]], axis=-1)
    return tensor * cosine + turn_sign * turned * sine_table


def dot_nn(a, b):
    return lax.dot_general(a, b, (((1,), (0,)), ((), ())), preferred_element_type=F32)


def dot_nt(a, b):
    return lax.dot_general(a, b, (((1,), (1,)), ((), ())), preferred_element_type=F32)


def dot_tn(a, b):
    return lax.dot_general(a, b, (((0,), (0,)), ((), ())), preferred_element_type=F32)


def pick(array, index):
    return lax.dynamic_index_in_dim(array, index, 0, keepdims=False)


def after(value, *others):
    return lax.optimization_barrier((value,) + others)[0]


def norm_back(tensor, inv_scale, gain_row, upstream):
    scaled = upstream * gain_row
    average = jnp.mean(scaled * tensor, axis=-1, keepdims=True)
    grad_tensor = inv_scale * scaled - tensor * (inv_scale * inv_scale * inv_scale) * average
    gain_term = jnp.sum(upstream * tensor * inv_scale, axis=0)
    return grad_tensor, gain_term


class Comm:
    def __init__(self, group=8):
        rows, seq = lax.axis_size("rows"), lax.axis_size("seq")
        self.part = max(1, min(rows, group // seq))
        self.copies, self.size, self.count = rows // self.part, self.part * seq, rows * seq
        row, s = lax.axis_index("rows"), lax.axis_index("seq")
        self.d = row // self.part
        self.g = (row % self.part) * seq + s
        self.seq, self.t, self.s = seq, row % self.part, s
        bits = [1 << i for i in range(self.size.bit_length() - 1)]
        self.bits = bits
        self.lines = [[i * self.size + g for i in range(self.copies)] for g in range(self.size)]
        self.order = list(range(0, self.size, 2)) + list(range(1, self.size, 2))

    def send(self, v, pairs):
        return lax.ppermute(v, ("rows", "seq"), pairs)

    def swap(self, v, j):
        return self.send(v, [(i, i ^ j) for i in range(self.count)])

    def gather(self, block):
        return lax.all_gather(block, ("rows", "seq"), axis=0, tiled=True, axis_index_groups=self.lines)

    def scatter(self, parts):
        return lax.psum_scatter(
            parts, ("rows", "seq"), scatter_dimension=0, tiled=True, axis_index_groups=self.lines
        )

    def exchange(self, parts, tokens=False):
        swap = self.swap if not tokens else lambda v, j: self.swap_tokens(v, j, 1)
        return self.exchange_chips(self.exchange_pair(parts, swap), swap)

    def exchange_pair(self, parts, swap):
        parts = parts.reshape((self.size // 2, 2) + parts.shape[1:])
        core = self.g % 2
        other = swap(lax.dynamic_index_in_dim(parts, 1 - core, 1, keepdims=False), 1)
        return lax.dynamic_update_index_in_dim(parts, other, 1 - core, 1)

    def exchange_chips(self, parts, swap):
        pair = self.g // 2
        picks = lax.optimization_barrier([pick(parts, pair ^ j) for j in range(1, self.size // 2)])
        moved = lax.optimization_barrier([swap(v, 2 * (j + 1)) for j, v in enumerate(picks)])
        for j, v in enumerate(moved):
            parts = lax.dynamic_update_index_in_dim(parts, v, pair ^ (j + 1), 0)
        return parts.reshape((self.size,) + parts.shape[2:])

    def swap_tokens(self, v, j, axis=0):
        pieces = jnp.split(self.swap(v, j), self.size, axis=axis)
        place = {k: p for p, k in enumerate(self.order)}
        return jnp.concatenate([pieces[place[k ^ j]] for k in self.order], axis=axis)

    def gather_tokens(self, v):
        got = {0: v}
        if self.size == 8:
            half = v.shape[0] // 2
            got[4], got[2] = self.swap(v, 4), self.swap(v, 2)
            got[1] = self.swap(v, 1)
            got[6] = jnp.concatenate([self.swap(got[4][:half], 2), self.swap(got[2][half:], 4)], axis=0)
            for k in (2, 4, 6):
                got[k + 1] = self.swap(got[k], 1)
        else:
            for bit in self.bits[::-1]:
                for k in sorted(got):
                    got[k | bit] = self.swap(got[k], bit)
        return jnp.concatenate([got[k] for k in self.order], axis=0)

    def scatter_tokens(self, tokens, make_dot):
        n = tokens.shape[0] // 2
        away = make_dot(tokens[n:]).astype(BF)
        m = n // (self.size // 2)
        moved = [self.swap(away[k * m : (k + 1) * m], 1) for k in range(self.size // 2)]
        kept = make_dot(tokens[:n])
        have = {2 * k: kept[k * m : (k + 1) * m] + moved[k].astype(F32) for k in range(self.size // 2)}
        if self.size == 8:
            half = m // 2
            last = have[6].astype(BF)
            four, two = self.swap(last[half:], 2), self.swap(last[:half], 4)
            mid4, mid2 = have[4].astype(BF), have[2].astype(BF)
            add4 = (have[4][half:] + four.astype(F32)).astype(BF)
            add2 = (have[2][:half] + two.astype(F32)).astype(BF)
            a = jnp.concatenate([self.swap(mid4[:half], 4), self.swap(add4, 4)], axis=0)
            b = jnp.concatenate([self.swap(add2, 2), self.swap(mid2[half:], 2)], axis=0)
            return have[0] + a.astype(F32) + b.astype(F32)
        for bit in self.bits[1:]:
            for k in [k for k in have if k & bit]:
                have[k ^ bit] = have[k ^ bit] + self.swap(have.pop(k).astype(BF), bit).astype(F32)
        return have[0]

    def sum_tokens(self, v):
        for bit in self.bits:
            v = v + self.swap_tokens(v, bit, 1)
        return v

    def sum_all(self, v):
        bit = 1
        while bit < self.count:
            v = v + self.swap(v, bit)
            bit *= 2
        return v


def per_device(layer_input, doc_lengths, w_qkv, w_out, w_gate_up, w_down, norm_gains, cotangent):
    c = Comm()
    copies, size, part = c.copies, c.size, c.part
    _, tl, d = layer_input.shape
    toks, row_len = tl * size, tl * c.seq
    heads = d // HD
    hl = heads // size
    wide = hl * HD
    n_in, n_out, n_ff = w_qkv.shape[0], w_out.shape[0], w_down.shape[0]
    ffl = n_ff * copies
    flat_in = layer_input.reshape(tl, d)
    pairs = 2 * n_out == HD and 2 * hl == copies
    half_group = size // 2

    lengths = doc_lengths.astype(jnp.int32)
    lengths = [lengths] + [c.swap(lengths, j * c.seq) for j in range(1, part)]
    lengths = jnp.concatenate(lengths, axis=0)

    if pairs:
        send_qkv = w_qkv.reshape(n_in, 3, 2, hl, half_group, HD).transpose(4, 2, 0, 1, 3, 5)
    else:
        send_qkv = w_qkv.reshape(n_in, 3, size, wide).transpose(2, 0, 1, 3)
    slab_qkv = c.exchange(send_qkv.reshape(size, n_in, 3 * wide)).reshape(size * n_in, 3 * wide)
    full_qkv = c.gather(slab_qkv)
    full_out = c.gather(w_out)
    x_full = c.gather_tokens(after(flat_in, slab_qkv, lengths))
    send_gu = w_gate_up.reshape(n_in, 2, copies, size, n_ff).transpose(3, 0, 1, 2, 4)
    send_gu = after(send_gu.reshape(size, n_in, 2 * ffl), x_full)
    slab_gu = c.exchange(send_gu).reshape(size * n_in, 2 * ffl)
    x_full, slab_gu = lax.optimization_barrier((x_full, slab_gu))
    full_gu = c.gather(slab_gu)
    full_down = c.gather(after(w_down, full_qkv))

    lengths = after(lengths, x_full)
    doc_ends = jnp.cumsum(lengths, axis=1)
    near = [k % c.seq for k in c.order if k < c.seq]
    places = jnp.concatenate([(c.s ^ k) * tl + jnp.arange(tl, dtype=jnp.int32) for k in near])
    passed = (places[None, :, None] >= doc_ends[:, None, :]).astype(jnp.int32)
    segment = jnp.sum(passed, axis=-1)
    positions = places[None, :] - jnp.sum(passed * lengths[:, None, :], axis=-1)
    allowed = (places[:, None] >= places[None, :])[None] & (segment[:, :, None] == segment[:, None, :])

    def by_rows(v):
        v = jnp.stack([v[:, k * HD : (k + 1) * HD] for k in range(v.shape[1] // HD)])
        v = v.reshape(-1, 2, part, c.seq // 2, tl, HD).transpose(2, 0, 1, 3, 4, 5)
        return v.reshape(part, -1, row_len, HD)

    def by_tokens(v):
        v = jnp.concatenate([v[:, k] for k in range(v.shape[1])], axis=-1)
        v = v.reshape(part, 2, c.seq // 2, tl, v.shape[-1]).swapaxes(0, 1)
        return v.reshape(toks, v.shape[-1])

    def stat_rows(v):
        v = v.reshape(-1, 2, part, c.seq // 2, tl).swapaxes(1, 2)
        return v.reshape(-1, part, 1, row_len, 1)

    def stat_tokens(v):
        v = v.reshape(-1, part, 2, c.seq // 2, tl).swapaxes(1, 2)
        return v.reshape(-1, toks)

    cosine, sine_table = rope_tables(positions.reshape(-1))
    cosine = cosine.reshape(part, 1, row_len, HD)
    sine_table = sine_table.reshape(part, 1, row_len, HD)
    if pairs:
        gains4 = norm_gains.reshape(4, 2, hl, half_group, HD).transpose(3, 1, 0, 2, 4).reshape(size, 4, wide)
    else:
        gains4 = norm_gains.reshape(4, size, wide).transpose(1, 0, 2)
    gains_own = pick(gains4, c.g)

    mixed = dot_nn(x_full, full_qkv)
    query_pre, key_pre = mixed[:, :wide], mixed[:, wide : 2 * wide]
    squares = jnp.stack([jnp.sum(query_pre * query_pre, -1), jnp.sum(key_pre * key_pre, -1)])
    scales = lax.rsqrt(c.sum_tokens(squares) / d + eps)
    query_scale, key_scale = stat_rows(scales)
    query_pre, key_pre = by_rows(query_pre), by_rows(key_pre)
    gain_q = gains_own[0].reshape(1, hl, 1, HD)
    gain_k = gains_own[1].reshape(1, hl, 1, HD)
    query = rotate(query_pre * query_scale * gain_q, cosine, sine_table, 1.0).astype(BF)
    key = rotate(key_pre * key_scale * gain_k, cosine, sine_table, 1.0).astype(BF)
    value = by_rows(mixed[:, 2 * wide :].astype(BF))
    score_scale = 1.0 / HD**0.5
    scores = jnp.einsum("rhqd,rhkd->rhqk", query, key, preferred_element_type=F32) * score_scale
    scores = jnp.where(allowed[:, None], scores, -1e30)
    row_max = jnp.max(scores, axis=-1, keepdims=True)
    exponent = jnp.exp(scores - row_max)
    probs = exponent / jnp.sum(exponent, axis=-1, keepdims=True)
    probs_low = probs.astype(BF)
    attended = jnp.einsum("rhqk,rhkd->rhqd", probs_low, value, preferred_element_type=F32).astype(BF)

    part_of = HD // 2

    def to_out(v):
        if pairs:
            core = c.g % 2
            cuts = [v[:, k * part_of : (k + 1) * part_of] for k in range(2 * hl)]
            v = jnp.stack([jnp.concatenate(cuts[0::2], axis=1), jnp.concatenate(cuts[1::2], axis=1)])
            own, got = pick(v, core), c.swap_tokens(pick(v, 1 - core), 1)
            first = jnp.where(core == 0, own, got)
            second = jnp.where(core == 0, got, own)
            return jnp.concatenate([first, second], axis=1)
        v = v.reshape(toks, wide // (size * n_out), size, n_out)
        v = c.exchange(v.transpose(2, 0, 1, 3).reshape(size, toks, wide // size), True)
        return v.transpose(1, 0, 2).reshape(toks, wide)

    def from_out(v):
        if pairs:
            core = c.g % 2
            v = jnp.stack([v[:, : wide // 2], v[:, wide // 2 :]])
            own, got = pick(v, core), c.swap_tokens(pick(v, 1 - core), 1)
            halves = [jnp.where(core == 0, own, got), jnp.where(core == 0, got, own)]
            cuts = [u[:, k * part_of : (k + 1) * part_of] for k in range(hl) for u in halves]
            return jnp.concatenate(cuts, axis=1)
        v = c.exchange(v.reshape(toks, size, wide // size).transpose(1, 0, 2), True)
        v = v.reshape(size, toks, wide // (size * n_out), n_out).transpose(1, 2, 0, 3)
        return v.reshape(toks, wide)

    attended = to_out(by_tokens(attended))
    branch = c.scatter_tokens(attended, lambda v: dot_nn(v, full_out))
    branch_scale = lax.rsqrt(jnp.mean(branch * branch, axis=-1, keepdims=True) + eps)
    hidden = flat_in.astype(F32) + branch * branch_scale * norm_gains[2]
    hidden_low = c.gather_tokens(hidden.astype(BF))

    gate_up = dot_nn(hidden_low, full_gu)
    gate, up = gate_up[:, :ffl], gate_up[:, ffl:]
    sig = jax.nn.sigmoid(gate)
    inner = (gate * sig * up).astype(BF)
    branch2 = c.scatter_tokens(inner, lambda v: dot_nn(v, full_down))
    branch2_scale = lax.rsqrt(jnp.mean(branch2 * branch2, axis=-1, keepdims=True) + eps)
    output = (hidden + branch2 * branch2_scale * norm_gains[3]).astype(BF)

    upstream = cotangent.reshape(tl, d).astype(F32)
    grad_branch2, gain_mlp = norm_back(branch2, branch2_scale, norm_gains[3], upstream)
    grad_branch2 = c.gather_tokens(grad_branch2.astype(BF))
    g_down = dot_tn(inner, grad_branch2).astype(BF)
    sum_down = c.scatter(g_down)
    grad_inner = dot_nt(after(grad_branch2, g_down), full_down)
    grad_gate = grad_inner * up * sig * (1.0 + gate * (1.0 - sig))
    grad_gu = jnp.concatenate([grad_gate, grad_inner * (gate * sig)], axis=1).astype(BF)
    grad_hidden = upstream + c.scatter_tokens(grad_gu, lambda v: dot_nt(v, full_gu))
    g_gu = dot_tn(hidden_low, grad_gu).astype(BF)
    sum_gu = c.scatter(g_gu)
    grad_branch, gain_attn = norm_back(branch, branch_scale, norm_gains[2], grad_hidden)
    grad_branch = c.gather_tokens(grad_branch.astype(BF))
    grad_branch = after(grad_branch, sum_down)
    g_out = dot_tn(attended, grad_branch).astype(BF)
    sum_out = c.scatter(g_out)
    grad_att = by_rows(from_out(dot_nt(grad_branch, full_out).astype(BF)))
    grad_probs = jnp.einsum("rhqd,rhkd->rhqk", grad_att, value, preferred_element_type=F32)
    grad_value = jnp.einsum("rhqk,rhqd->rhkd", probs_low, grad_att, preferred_element_type=F32)
    row_sum = jnp.sum(probs * grad_probs, axis=-1, keepdims=True)
    grad_scores = (probs * (grad_probs - row_sum)).astype(BF)
    grad_query = jnp.einsum("rhqk,rhkd->rhqd", grad_scores, key, preferred_element_type=F32)
    grad_key = jnp.einsum("rhqk,rhqd->rhkd", grad_scores, query, preferred_element_type=F32)
    grad_query = (grad_query * score_scale).astype(BF).astype(F32)
    grad_key = (grad_key * score_scale).astype(BF).astype(F32)
    e_query = rotate(grad_query, cosine, sine_table, -1.0)
    e_key = rotate(grad_key, cosine, sine_table, -1.0)
    scaled_q, scaled_k = e_query * gain_q, e_key * gain_k
    sums = jnp.stack(
        [jnp.sum(scaled_q * query_pre, axis=(1, 3)), jnp.sum(scaled_k * key_pre, axis=(1, 3))]
    )
    mean_q, mean_k = stat_rows(c.sum_tokens(stat_tokens(sums)) / d)
    grad_qp = query_scale * scaled_q - query_pre * query_scale**3 * mean_q
    grad_kp = key_scale * scaled_k - key_pre * key_scale**3 * mean_k
    gain_query = jnp.sum(e_query * query_pre * query_scale, axis=(0, 2)).reshape(wide)
    gain_key = jnp.sum(e_key * key_pre * key_scale, axis=(0, 2)).reshape(wide)
    grad_mixed = by_tokens(
        jnp.concatenate([grad_qp.astype(BF), grad_kp.astype(BF), grad_value.astype(BF)], axis=1)
    )
    back_gu = c.exchange_pair(sum_gu.reshape(size, n_in, 2 * ffl), c.swap)
    grad_mixed = after(grad_mixed, back_gu)
    g_qkv = dot_tn(x_full, grad_mixed).astype(BF)
    sum_qkv = c.scatter(g_qkv)
    back_gu = c.exchange_chips(back_gu, c.swap)
    grad_mixed = after(grad_mixed, g_qkv, back_gu)
    grad_input = grad_hidden + c.scatter_tokens(grad_mixed, lambda v: dot_nt(v, full_qkv))
    back_gu = back_gu.astype(F32).reshape(size, n_in, 2, copies, n_ff)
    grad_gate_up = back_gu.transpose(1, 2, 3, 0, 4)
    back_qkv = c.exchange(sum_qkv.reshape(size, n_in, 3 * wide)).astype(F32)
    if pairs:
        grad_qkv = back_qkv.reshape(half_group, 2, n_in, 3, hl, HD).transpose(2, 3, 1, 4, 0, 5)
    else:
        grad_qkv = back_qkv.reshape(size, n_in, 3, wide).transpose(1, 2, 0, 3)

    own_terms = jnp.zeros((size, 2, wide), F32)
    own_terms = lax.dynamic_update_slice(own_terms, jnp.stack([gain_query, gain_key])[None], (c.g, 0, 0))
    if pairs:
        own_terms = own_terms.reshape(half_group, 2, 2, hl, HD).transpose(2, 1, 3, 0, 4)
    else:
        own_terms = own_terms.transpose(1, 0, 2)
    terms = jnp.concatenate([own_terms.reshape(2, d), jnp.stack([gain_attn, gain_mlp])])
    grad_gains = c.sum_all(terms)

    return (
        output.reshape(layer_input.shape),
        grad_input.reshape(layer_input.shape),
        grad_qkv.reshape(w_qkv.shape),
        sum_out.astype(F32),
        grad_gate_up.reshape(w_gate_up.shape),
        sum_down.astype(F32),
        grad_gains,
    )


def solution(mesh):
    both = P(("rows", "seq"), None)
    tokens = P("rows", "seq", None)
    return jax.shard_map(
        per_device,
        mesh=mesh,
        in_specs=(tokens, P("rows", None), both, both, both, both, P(), tokens),
        out_specs=(tokens, tokens, both, both, both, both, P()),
        check_vma=False,
    )
```

```python
import jax
import jax.numpy as jnp
from jax import lax
from jax.sharding import PartitionSpec as P

HD = 128
BF = jnp.bfloat16
F32 = jnp.float32

eps = 1e-06
rope_base = 500000.0


def rope_tables(positions):
    half_width = HD // 2
    frequency = jnp.power(rope_base, -(jnp.arange(half_width, dtype=F32) * 2.0) / HD)
    angles = positions.astype(F32)[:, None] * frequency
    cosine, sine_table = lax.optimization_barrier((jnp.cos(angles), jnp.sin(angles)))
    cosine = jnp.concatenate([cosine, cosine], axis=-1)
    sine_table = jnp.concatenate([sine_table, sine_table], axis=-1)
    return cosine[:, None, :], sine_table[:, None, :]


def rotate(tensor, cosine, sine_table, turn_sign):
    half_width = HD // 2
    turned = jnp.concatenate([-tensor[..., half_width:], tensor[..., :half_width]], axis=-1)
    return tensor * cosine + turn_sign * turned * sine_table


def dot_nn(a, b):
    return lax.dot_general(a, b, (((1,), (0,)), ((), ())), preferred_element_type=F32)


def dot_nt(a, b):
    return lax.dot_general(a, b, (((1,), (1,)), ((), ())), preferred_element_type=F32)


def dot_tn(a, b):
    return lax.dot_general(a, b, (((0,), (0,)), ((), ())), preferred_element_type=F32)


def pick(array, index):
    return lax.dynamic_index_in_dim(array, index, 0, keepdims=False)


def after(value, *others):
    return lax.optimization_barrier((value,) + others)[0]


def norm_back(tensor, inv_scale, gain_row, upstream):
    scaled = upstream * gain_row
    average = jnp.mean(scaled * tensor, axis=-1, keepdims=True)
    grad_tensor = inv_scale * scaled - tensor * (inv_scale * inv_scale * inv_scale) * average
    gain_term = jnp.sum(upstream * tensor * inv_scale, axis=0)
    return grad_tensor, gain_term


class Comm:
    def __init__(self, group=8):
        rows, seq = lax.axis_size("rows"), lax.axis_size("seq")
        self.part = max(1, min(rows, group // seq))
        self.copies, self.size, self.count = rows // self.part, self.part * seq, rows * seq
        row, s = lax.axis_index("rows"), lax.axis_index("seq")
        self.d = row // self.part
        self.g = (row % self.part) * seq + s
        self.seq, self.t, self.s = seq, row % self.part, s
        bits = [1 << i for i in range(self.size.bit_length() - 1)]
        self.bits = bits
        self.lines = [[i * self.size + g for i in range(self.copies)] for g in range(self.size)]
        self.order = list(range(0, self.size, 2)) + list(range(1, self.size, 2))

    def send(self, v, pairs):
        return lax.ppermute(v, ("rows", "seq"), pairs)

    def swap(self, v, j):
        return self.send(v, [(i, i ^ j) for i in range(self.count)])

    def gather(self, block):
        return lax.all_gather(block, ("rows", "seq"), axis=0, tiled=True, axis_index_groups=self.lines)

    def scatter(self, parts):
        return lax.psum_scatter(
            parts, ("rows", "seq"), scatter_dimension=0, tiled=True, axis_index_groups=self.lines
        )

    def exchange(self, parts, tokens=False):
        swap = self.swap if not tokens else lambda v, j: self.swap_tokens(v, j, 1)
        return self.exchange_chips(self.exchange_pair(parts, swap), swap)

    def exchange_pair(self, parts, swap):
        parts = parts.reshape((self.size // 2, 2) + parts.shape[1:])
        core = self.g % 2
        other = swap(lax.dynamic_index_in_dim(parts, 1 - core, 1, keepdims=False), 1)
        return lax.dynamic_update_index_in_dim(parts, other, 1 - core, 1)

    def exchange_chips(self, parts, swap):
        pair = self.g // 2
        picks = lax.optimization_barrier([pick(parts, pair ^ j) for j in range(1, self.size // 2)])
        moved = lax.optimization_barrier([swap(v, 2 * (j + 1)) for j, v in enumerate(picks)])
        for j, v in enumerate(moved):
            parts = lax.dynamic_update_index_in_dim(parts, v, pair ^ (j + 1), 0)
        return parts.reshape((self.size,) + parts.shape[2:])

    def swap_tokens(self, v, j, axis=0):
        pieces = jnp.split(self.swap(v, j), self.size, axis=axis)
        place = {k: p for p, k in enumerate(self.order)}
        return jnp.concatenate([pieces[place[k ^ j]] for k in self.order], axis=axis)

    def gather_tokens(self, v):
        got = {0: v}
        if self.size == 8:
            half = v.shape[0] // 2
            got[4], got[2] = self.swap(v, 4), self.swap(v, 2)
            got[1] = self.swap(v, 1)
            got[6] = jnp.concatenate([self.swap(got[4][:half], 2), self.swap(got[2][half:], 4)], axis=0)
            for k in (2, 4, 6):
                got[k + 1] = self.swap(got[k], 1)
        else:
            for bit in self.bits[::-1]:
                for k in sorted(got):
                    got[k | bit] = self.swap(got[k], bit)
        return jnp.concatenate([got[k] for k in self.order], axis=0)

    def scatter_tokens(self, tokens, make_dot):
        n = tokens.shape[0] // 2
        away = make_dot(tokens[n:]).astype(BF)
        m = n // (self.size // 2)
        moved = [self.swap(away[k * m : (k + 1) * m], 1) for k in range(self.size // 2)]
        kept = make_dot(tokens[:n])
        have = {2 * k: kept[k * m : (k + 1) * m] + moved[k].astype(F32) for k in range(self.size // 2)}
        if self.size == 8:
            half = m // 2
            last = have[6].astype(BF)
            four, two = self.swap(last[half:], 2), self.swap(last[:half], 4)
            mid4, mid2 = have[4].astype(BF), have[2].astype(BF)
            add4 = (have[4][half:] + four.astype(F32)).astype(BF)
            add2 = (have[2][:half] + two.astype(F32)).astype(BF)
            a = jnp.concatenate([self.swap(mid4[:half], 4), self.swap(add4, 4)], axis=0)
            b = jnp.concatenate([self.swap(add2, 2), self.swap(mid2[half:], 2)], axis=0)
            return have[0] + a.astype(F32) + b.astype(F32)
        for bit in self.bits[1:]:
            for k in [k for k in have if k & bit]:
                have[k ^ bit] = have[k ^ bit] + self.swap(have.pop(k).astype(BF), bit).astype(F32)
        return have[0]

    def sum_tokens(self, v):
        for bit in self.bits:
            v = v + self.swap_tokens(v, bit, 1)
        return v

    def sum_all(self, v):
        bit = 1
        while bit < self.count:
            v = v + self.swap(v, bit)
            bit *= 2
        return v


def per_device(layer_input, doc_lengths, w_qkv, w_out, w_gate_up, w_down, norm_gains, cotangent):
    c = Comm()
    copies, size, part = c.copies, c.size, c.part
    _, tl, d = layer_input.shape
    toks, row_len = tl * size, tl * c.seq
    heads = d // HD
    hl = heads // size
    wide = hl * HD
    n_in, n_out, n_ff = w_qkv.shape[0], w_out.shape[0], w_down.shape[0]
    ffl = n_ff * copies
    flat_in = layer_input.reshape(tl, d)
    pairs = 2 * n_out == HD and 2 * hl == copies
    half_group = size // 2

    lengths = doc_lengths.astype(jnp.int32)
    lengths = [lengths] + [c.swap(lengths, j * c.seq) for j in range(1, part)]
    lengths = jnp.concatenate(lengths, axis=0)

    if pairs:
        send_qkv = w_qkv.reshape(n_in, 3, 2, hl, half_group, HD).transpose(4, 2, 0, 1, 3, 5)
    else:
        send_qkv = w_qkv.reshape(n_in, 3, size, wide).transpose(2, 0, 1, 3)
    slab_qkv = c.exchange(send_qkv.reshape(size, n_in, 3 * wide)).reshape(size * n_in, 3 * wide)
    full_qkv = c.gather(slab_qkv)
    full_out = c.gather(w_out)
    x_full = c.gather_tokens(after(flat_in, slab_qkv, lengths))
    send_gu = w_gate_up.reshape(n_in, 2, copies, size, n_ff).transpose(3, 0, 1, 2, 4)
    send_gu = after(send_gu.reshape(size, n_in, 2 * ffl), x_full)
    slab_gu = c.exchange(send_gu).reshape(size * n_in, 2 * ffl)
    x_full, slab_gu = lax.optimization_barrier((x_full, slab_gu))
    full_gu = c.gather(slab_gu)
    full_down = c.gather(after(w_down, full_qkv))

    lengths = after(lengths, x_full)
    doc_ends = jnp.cumsum(lengths, axis=1)
    near = [k % c.seq for k in c.order if k < c.seq]
    places = jnp.concatenate([(c.s ^ k) * tl + jnp.arange(tl, dtype=jnp.int32) for k in near])
    passed = (places[None, :, None] >= doc_ends[:, None, :]).astype(jnp.int32)
    segment = jnp.sum(passed, axis=-1)
    positions = places[None, :] - jnp.sum(passed * lengths[:, None, :], axis=-1)
    allowed = (places[:, None] >= places[None, :])[None] & (segment[:, :, None] == segment[:, None, :])

    def by_rows(v):
        v = jnp.stack([v[:, k * HD : (k + 1) * HD] for k in range(v.shape[1] // HD)])
        v = v.reshape(-1, 2, part, c.seq // 2, tl, HD).transpose(2, 0, 1, 3, 4, 5)
        return v.reshape(part, -1, row_len, HD)

    def by_tokens(v):
        v = jnp.concatenate([v[:, k] for k in range(v.shape[1])], axis=-1)
        v = v.reshape(part, 2, c.seq // 2, tl, v.shape[-1]).swapaxes(0, 1)
        return v.reshape(toks, v.shape[-1])

    def stat_rows(v):
        v = v.reshape(-1, 2, part, c.seq // 2, tl).swapaxes(1, 2)
        return v.reshape(-1, part, 1, row_len, 1)

    def stat_tokens(v):
        v = v.reshape(-1, part, 2, c.seq // 2, tl).swapaxes(1, 2)
        return v.reshape(-1, toks)

    cosine, sine_table = rope_tables(positions.reshape(-1))
    cosine = cosine.reshape(part, 1, row_len, HD)
    sine_table = sine_table.reshape(part, 1, row_len, HD)
    if pairs:
        gains4 = norm_gains.reshape(4, 2, hl, half_group, HD).transpose(3, 1, 0, 2, 4).reshape(size, 4, wide)
    else:
        gains4 = norm_gains.reshape(4, size, wide).transpose(1, 0, 2)
    gains_own = pick(gains4, c.g)

    mixed = dot_nn(x_full, full_qkv)
    query_pre, key_pre = mixed[:, :wide], mixed[:, wide : 2 * wide]
    squares = jnp.stack([jnp.sum(query_pre * query_pre, -1), jnp.sum(key_pre * key_pre, -1)])
    scales = lax.rsqrt(c.sum_tokens(squares) / d + eps)
    query_scale, key_scale = stat_rows(scales)
    query_pre, key_pre = by_rows(query_pre), by_rows(key_pre)
    gain_q = gains_own[0].reshape(1, hl, 1, HD)
    gain_k = gains_own[1].reshape(1, hl, 1, HD)
    query = rotate(query_pre * query_scale * gain_q, cosine, sine_table, 1.0).astype(BF)
    key = rotate(key_pre * key_scale * gain_k, cosine, sine_table, 1.0).astype(BF)
    value = by_rows(mixed[:, 2 * wide :].astype(BF))
    score_scale = 1.0 / HD**0.5
    scores = jnp.einsum("rhqd,rhkd->rhqk", query, key, preferred_element_type=F32) * score_scale
    scores = jnp.where(allowed[:, None], scores, -1e30)
    row_max = jnp.max(scores, axis=-1, keepdims=True)
    exponent = jnp.exp(scores - row_max)
    probs = exponent / jnp.sum(exponent, axis=-1, keepdims=True)
    probs_low = probs.astype(BF)
    attended = jnp.einsum("rhqk,rhkd->rhqd", probs_low, value, preferred_element_type=F32).astype(BF)

    part_of = HD // 2

    def to_out(v):
        if pairs:
            core = c.g % 2
            cuts = [v[:, k * part_of : (k + 1) * part_of] for k in range(2 * hl)]
            v = jnp.stack([jnp.concatenate(cuts[0::2], axis=1), jnp.concatenate(cuts[1::2], axis=1)])
            own, got = pick(v, core), c.swap_tokens(pick(v, 1 - core), 1)
            first = jnp.where(core == 0, own, got)
            second = jnp.where(core == 0, got, own)
            return jnp.concatenate([first, second], axis=1)
        v = v.reshape(toks, wide // (size * n_out), size, n_out)
        v = c.exchange(v.transpose(2, 0, 1, 3).reshape(size, toks, wide // size), True)
        return v.transpose(1, 0, 2).reshape(toks, wide)

    def from_out(v):
        if pairs:
            core = c.g % 2
            v = jnp.stack([v[:, : wide // 2], v[:, wide // 2 :]])
            own, got = pick(v, core), c.swap_tokens(pick(v, 1 - core), 1)
            halves = [jnp.where(core == 0, own, got), jnp.where(core == 0, got, own)]
            cuts = [u[:, k * part_of : (k + 1) * part_of] for k in range(hl) for u in halves]
            return jnp.concatenate(cuts, axis=1)
        v = c.exchange(v.reshape(toks, size, wide // size).transpose(1, 0, 2), True)
        v = v.reshape(size, toks, wide // (size * n_out), n_out).transpose(1, 2, 0, 3)
        return v.reshape(toks, wide)

    attended = to_out(by_tokens(attended))
    branch = c.scatter_tokens(attended, lambda v: dot_nn(v, full_out))
    branch_scale = lax.rsqrt(jnp.mean(branch * branch, axis=-1, keepdims=True) + eps)
    hidden = flat_in.astype(F32) + branch * branch_scale * norm_gains[2]
    hidden_low = c.gather_tokens(hidden.astype(BF))

    gate_up = dot_nn(hidden_low, full_gu)
    gate, up = gate_up[:, :ffl], gate_up[:, ffl:]
    sig = jax.nn.sigmoid(gate)
    inner = (gate * sig * up).astype(BF)
    branch2 = c.scatter_tokens(inner, lambda v: dot_nn(v, full_down))
    branch2_scale = lax.rsqrt(jnp.mean(branch2 * branch2, axis=-1, keepdims=True) + eps)
    output = (hidden + branch2 * branch2_scale * norm_gains[3]).astype(BF)

    upstream = cotangent.reshape(tl, d).astype(F32)
    grad_branch2, gain_mlp = norm_back(branch2, branch2_scale, norm_gains[3], upstream)
    grad_branch2 = c.gather_tokens(grad_branch2.astype(BF))
    g_down = dot_tn(inner, grad_branch2).astype(BF)
    sum_down = c.scatter(g_down)
    grad_inner = dot_nt(after(grad_branch2, g_down), full_down)
    grad_gate = grad_inner * up * sig * (1.0 + gate * (1.0 - sig))
    grad_gu = jnp.concatenate([grad_gate, grad_inner * (gate * sig)], axis=1).astype(BF)
    grad_hidden = upstream + c.scatter_tokens(grad_gu, lambda v: dot_nt(v, full_gu))
    g_gu = dot_tn(hidden_low, grad_gu).astype(BF)
    sum_gu = c.scatter(g_gu)
    grad_branch, gain_attn = norm_back(branch, branch_scale, norm_gains[2], grad_hidden)
    grad_branch = c.gather_tokens(grad_branch.astype(BF))
    grad_branch = after(grad_branch, sum_down)
    g_out = dot_tn(attended, grad_branch).astype(BF)
    sum_out = c.scatter(g_out)
    grad_att = by_rows(from_out(dot_nt(grad_branch, full_out).astype(BF)))
    grad_probs = jnp.einsum("rhqd,rhkd->rhqk", grad_att, value, preferred_element_type=F32)
    grad_value = jnp.einsum("rhqk,rhqd->rhkd", probs_low, grad_att, preferred_element_type=F32)
    row_sum = jnp.sum(probs * grad_probs, axis=-1, keepdims=True)
    grad_scores = (probs * (grad_probs - row_sum)).astype(BF)
    grad_query = jnp.einsum("rhqk,rhkd->rhqd", grad_scores, key, preferred_element_type=F32)
    grad_key = jnp.einsum("rhqk,rhqd->rhkd", grad_scores, query, preferred_element_type=F32)
    grad_query = (grad_query * score_scale).astype(BF).astype(F32)
    grad_key = (grad_key * score_scale).astype(BF).astype(F32)
    e_query = rotate(grad_query, cosine, sine_table, -1.0)
    e_key = rotate(grad_key, cosine, sine_table, -1.0)
    scaled_q, scaled_k = e_query * gain_q, e_key * gain_k
    sums = jnp.stack(
        [jnp.sum(scaled_q * query_pre, axis=(1, 3)), jnp.sum(scaled_k * key_pre, axis=(1, 3))]
    )
    mean_q, mean_k = stat_rows(c.sum_tokens(stat_tokens(sums)) / d)
    grad_qp = query_scale * scaled_q - query_pre * query_scale**3 * mean_q
    grad_kp = key_scale * scaled_k - key_pre * key_scale**3 * mean_k
    gain_query = jnp.sum(e_query * query_pre * query_scale, axis=(0, 2)).reshape(wide)
    gain_key = jnp.sum(e_key * key_pre * key_scale, axis=(0, 2)).reshape(wide)
    own_terms = jnp.zeros((size, 2, wide), F32)
    own_terms = lax.dynamic_update_slice(own_terms, jnp.stack([gain_query, gain_key])[None], (c.g, 0, 0))
    if pairs:
        own_terms = own_terms.reshape(half_group, 2, 2, hl, HD).transpose(2, 1, 3, 0, 4)
    else:
        own_terms = own_terms.transpose(1, 0, 2)
    terms = jnp.concatenate([own_terms.reshape(2, d), jnp.stack([gain_attn, gain_mlp])])
    grad_gains = c.sum_all(terms)
    grad_mixed = by_tokens(
        jnp.concatenate([grad_qp.astype(BF), grad_kp.astype(BF), grad_value.astype(BF)], axis=1)
    )
    back_gu = c.exchange_pair(sum_gu.reshape(size, n_in, 2 * ffl), c.swap)
    grad_mixed = after(grad_mixed, back_gu, grad_gains)
    g_qkv = dot_tn(x_full, grad_mixed).astype(BF)
    sum_qkv = c.scatter(g_qkv)
    back_gu = c.exchange_chips(back_gu, c.swap)
    grad_mixed = after(grad_mixed, g_qkv, back_gu)
    grad_input = grad_hidden + c.scatter_tokens(grad_mixed, lambda v: dot_nt(v, full_qkv))
    back_gu = back_gu.astype(F32).reshape(size, n_in, 2, copies, n_ff)
    grad_gate_up = back_gu.transpose(1, 2, 3, 0, 4)
    back_qkv = c.exchange(sum_qkv.reshape(size, n_in, 3 * wide)).astype(F32)
    if pairs:
        grad_qkv = back_qkv.reshape(half_group, 2, n_in, 3, hl, HD).transpose(2, 3, 1, 4, 0, 5)
    else:
        grad_qkv = back_qkv.reshape(size, n_in, 3, wide).transpose(1, 2, 0, 3)

    return (
        output.reshape(layer_input.shape),
        grad_input.reshape(layer_input.shape),
        grad_qkv.reshape(w_qkv.shape),
        sum_out.astype(F32),
        grad_gate_up.reshape(w_gate_up.shape),
        sum_down.astype(F32),
        grad_gains,
    )


def solution(mesh):
    both = P(("rows", "seq"), None)
    tokens = P("rows", "seq", None)
    return jax.shard_map(
        per_device,
        mesh=mesh,
        in_specs=(tokens, P("rows", None), both, both, both, both, P(), tokens),
        out_specs=(tokens, tokens, both, both, both, both, P()),
        check_vma=False,
    )
```

```python
import jax
import jax.numpy as jnp
from jax import lax
from jax.sharding import PartitionSpec as P

HD = 128
BF = jnp.bfloat16
F32 = jnp.float32

eps = 1e-06
rope_base = 500000.0


def rope_tables(positions):
    half_width = HD // 2
    frequency = jnp.power(rope_base, -(jnp.arange(half_width, dtype=F32) * 2.0) / HD)
    angles = positions.astype(F32)[:, None] * frequency
    cosine, sine_table = lax.optimization_barrier((jnp.cos(angles), jnp.sin(angles)))
    cosine = jnp.concatenate([cosine, cosine], axis=-1)
    sine_table = jnp.concatenate([sine_table, sine_table], axis=-1)
    return cosine[:, None, :], sine_table[:, None, :]


def rotate(tensor, cosine, sine_table, turn_sign):
    half_width = HD // 2
    turned = jnp.concatenate([-tensor[..., half_width:], tensor[..., :half_width]], axis=-1)
    return tensor * cosine + turn_sign * turned * sine_table


def dot_nn(a, b):
    return lax.dot_general(a, b, (((1,), (0,)), ((), ())), preferred_element_type=F32)


def dot_nt(a, b):
    return lax.dot_general(a, b, (((1,), (1,)), ((), ())), preferred_element_type=F32)


def dot_tn(a, b):
    return lax.dot_general(a, b, (((0,), (0,)), ((), ())), preferred_element_type=F32)


def pick(array, index):
    return lax.dynamic_index_in_dim(array, index, 0, keepdims=False)


def after(value, *others):
    return lax.optimization_barrier((value,) + others)[0]


def norm_back(tensor, inv_scale, gain_row, upstream):
    scaled = upstream * gain_row
    average = jnp.mean(scaled * tensor, axis=-1, keepdims=True)
    grad_tensor = inv_scale * scaled - tensor * (inv_scale * inv_scale * inv_scale) * average
    gain_term = jnp.sum(upstream * tensor * inv_scale, axis=0)
    return grad_tensor, gain_term


class Comm:
    def __init__(self, group=8):
        rows, seq = lax.axis_size("rows"), lax.axis_size("seq")
        self.part = max(1, min(rows, group // seq))
        self.copies, self.size, self.count = rows // self.part, self.part * seq, rows * seq
        row, s = lax.axis_index("rows"), lax.axis_index("seq")
        self.d = row // self.part
        self.g = (row % self.part) * seq + s
        self.seq, self.t, self.s = seq, row % self.part, s
        bits = [1 << i for i in range(self.size.bit_length() - 1)]
        self.bits = bits
        self.lines = [[i * self.size + g for i in range(self.copies)] for g in range(self.size)]
        self.order = list(range(0, self.size, 2)) + list(range(1, self.size, 2))

    def send(self, v, pairs):
        return lax.ppermute(v, ("rows", "seq"), pairs)

    def swap(self, v, j):
        return self.send(v, [(i, i ^ j) for i in range(self.count)])

    def gather(self, block):
        return lax.all_gather(block, ("rows", "seq"), axis=0, tiled=True, axis_index_groups=self.lines)

    def scatter(self, parts):
        return lax.psum_scatter(
            parts, ("rows", "seq"), scatter_dimension=0, tiled=True, axis_index_groups=self.lines
        )

    def exchange(self, parts, tokens=False):
        swap = self.swap if not tokens else lambda v, j: self.swap_tokens(v, j, 1)
        return self.exchange_chips(self.exchange_pair(parts, swap), swap)

    def exchange_pair(self, parts, swap):
        parts = parts.reshape((self.size // 2, 2) + parts.shape[1:])
        core = self.g % 2
        other = swap(lax.dynamic_index_in_dim(parts, 1 - core, 1, keepdims=False), 1)
        return lax.dynamic_update_index_in_dim(parts, other, 1 - core, 1)

    def exchange_chips(self, parts, swap):
        pair = self.g // 2
        picks = lax.optimization_barrier([pick(parts, pair ^ j) for j in range(1, self.size // 2)])
        moved = lax.optimization_barrier([swap(v, 2 * (j + 1)) for j, v in enumerate(picks)])
        for j, v in enumerate(moved):
            parts = lax.dynamic_update_index_in_dim(parts, v, pair ^ (j + 1), 0)
        return parts.reshape((self.size,) + parts.shape[2:])

    def swap_tokens(self, v, j, axis=0):
        pieces = jnp.split(self.swap(v, j), self.size, axis=axis)
        place = {k: p for p, k in enumerate(self.order)}
        return jnp.concatenate([pieces[place[k ^ j]] for k in self.order], axis=axis)

    def gather_tokens(self, v):
        got = {0: v}
        if self.size == 8:
            half = v.shape[0] // 2
            got[4], got[2] = self.swap(v, 4), self.swap(v, 2)
            got[1] = self.swap(v, 1)
            got[6] = jnp.concatenate([self.swap(got[4][:half], 2), self.swap(got[2][half:], 4)], axis=0)
            for k in (2, 4, 6):
                got[k + 1] = self.swap(got[k], 1)
        else:
            for bit in self.bits[::-1]:
                for k in sorted(got):
                    got[k | bit] = self.swap(got[k], bit)
        return jnp.concatenate([got[k] for k in self.order], axis=0)

    def scatter_tokens(self, tokens, make_dot):
        n = tokens.shape[0] // 2
        away = make_dot(tokens[n:]).astype(BF)
        m = n // (self.size // 2)
        moved = [self.swap(away[k * m : (k + 1) * m], 1) for k in range(self.size // 2)]
        kept = make_dot(tokens[:n])
        have = {2 * k: kept[k * m : (k + 1) * m] + moved[k].astype(F32) for k in range(self.size // 2)}
        if self.size == 8:
            half = m // 2
            last = have[6].astype(BF)
            four, two = self.swap(last[half:], 2), self.swap(last[:half], 4)
            mid4, mid2 = have[4].astype(BF), have[2].astype(BF)
            add4 = (have[4][half:] + four.astype(F32)).astype(BF)
            add2 = (have[2][:half] + two.astype(F32)).astype(BF)
            a = jnp.concatenate([self.swap(mid4[:half], 4), self.swap(add4, 4)], axis=0)
            b = jnp.concatenate([self.swap(add2, 2), self.swap(mid2[half:], 2)], axis=0)
            return have[0] + a.astype(F32) + b.astype(F32)
        for bit in self.bits[1:]:
            for k in [k for k in have if k & bit]:
                have[k ^ bit] = have[k ^ bit] + self.swap(have.pop(k).astype(BF), bit).astype(F32)
        return have[0]

    def sum_tokens(self, v):
        for bit in self.bits:
            v = v + self.swap_tokens(v, bit, 1)
        return v

    def sum_all(self, v):
        bit = 1
        while bit < self.count:
            v = v + self.swap(v, bit)
            bit *= 2
        return v


def per_device(layer_input, doc_lengths, w_qkv, w_out, w_gate_up, w_down, norm_gains, cotangent):
    c = Comm()
    copies, size, part = c.copies, c.size, c.part
    _, tl, d = layer_input.shape
    toks, row_len = tl * size, tl * c.seq
    heads = d // HD
    hl = heads // size
    wide = hl * HD
    n_in, n_out, n_ff = w_qkv.shape[0], w_out.shape[0], w_down.shape[0]
    ffl = n_ff * copies
    flat_in = layer_input.reshape(tl, d)
    pairs = 2 * n_out == HD and 2 * hl == copies
    half_group = size // 2

    lengths = doc_lengths.astype(jnp.int32)
    lengths = [lengths] + [c.swap(lengths, j * c.seq) for j in range(1, part)]
    lengths = jnp.concatenate(lengths, axis=0)

    if pairs:
        send_qkv = w_qkv.reshape(n_in, 3, 2, hl, half_group, HD).transpose(4, 2, 0, 1, 3, 5)
    else:
        send_qkv = w_qkv.reshape(n_in, 3, size, wide).transpose(2, 0, 1, 3)
    slab_qkv = c.exchange(send_qkv.reshape(size, n_in, 3 * wide)).reshape(size * n_in, 3 * wide)
    full_qkv = c.gather(slab_qkv)
    full_out = c.gather(w_out)
    x_full = c.gather_tokens(after(flat_in, slab_qkv, lengths))
    send_gu = w_gate_up.reshape(n_in, 2, copies, size, n_ff).transpose(3, 0, 1, 2, 4)
    send_gu = after(send_gu.reshape(size, n_in, 2 * ffl), x_full)
    slab_gu = c.exchange(send_gu).reshape(size * n_in, 2 * ffl)
    x_full, slab_gu = lax.optimization_barrier((x_full, slab_gu))
    full_gu = c.gather(slab_gu)
    full_down = c.gather(after(w_down, full_qkv))

    lengths = after(lengths, x_full)
    doc_ends = jnp.cumsum(lengths, axis=1)
    near = [k % c.seq for k in c.order if k < c.seq]
    places = jnp.concatenate([(c.s ^ k) * tl + jnp.arange(tl, dtype=jnp.int32) for k in near])
    passed = (places[None, :, None] >= doc_ends[:, None, :]).astype(jnp.int32)
    segment = jnp.sum(passed, axis=-1)
    positions = places[None, :] - jnp.sum(passed * lengths[:, None, :], axis=-1)
    allowed = (places[:, None] >= places[None, :])[None] & (segment[:, :, None] == segment[:, None, :])

    def by_rows(v):
        v = jnp.stack([v[:, k * HD : (k + 1) * HD] for k in range(v.shape[1] // HD)])
        v = v.reshape(-1, 2, part, c.seq // 2, tl, HD).transpose(2, 0, 1, 3, 4, 5)
        return v.reshape(part, -1, row_len, HD)

    def by_tokens(v):
        v = jnp.concatenate([v[:, k] for k in range(v.shape[1])], axis=-1)
        v = v.reshape(part, 2, c.seq // 2, tl, v.shape[-1]).swapaxes(0, 1)
        return v.reshape(toks, v.shape[-1])

    def stat_rows(v):
        v = v.reshape(-1, 2, part, c.seq // 2, tl).swapaxes(1, 2)
        return v.reshape(-1, part, 1, row_len, 1)

    def stat_tokens(v):
        v = v.reshape(-1, part, 2, c.seq // 2, tl).swapaxes(1, 2)
        return v.reshape(-1, toks)

    cosine, sine_table = rope_tables(positions.reshape(-1))
    cosine = cosine.reshape(part, 1, row_len, HD)
    sine_table = sine_table.reshape(part, 1, row_len, HD)
    if pairs:
        gains4 = norm_gains.reshape(4, 2, hl, half_group, HD).transpose(3, 1, 0, 2, 4).reshape(size, 4, wide)
    else:
        gains4 = norm_gains.reshape(4, size, wide).transpose(1, 0, 2)
    gains_own = pick(gains4, c.g)

    mixed = dot_nn(x_full, full_qkv)
    query_pre, key_pre = mixed[:, :wide], mixed[:, wide : 2 * wide]
    squares = jnp.stack([jnp.sum(query_pre * query_pre, -1), jnp.sum(key_pre * key_pre, -1)])
    scales = lax.rsqrt(c.sum_tokens(squares) / d + eps)
    query_scale, key_scale = stat_rows(scales)
    query_pre, key_pre = by_rows(query_pre), by_rows(key_pre)
    gain_q = gains_own[0].reshape(1, hl, 1, HD)
    gain_k = gains_own[1].reshape(1, hl, 1, HD)
    query = rotate(query_pre * query_scale * gain_q, cosine, sine_table, 1.0).astype(BF)
    key = rotate(key_pre * key_scale * gain_k, cosine, sine_table, 1.0).astype(BF)
    value = by_rows(mixed[:, 2 * wide :].astype(BF))
    score_scale = 1.0 / HD**0.5
    scores = jnp.einsum("rhqd,rhkd->rhqk", query, key, preferred_element_type=F32) * score_scale
    scores = jnp.where(allowed[:, None], scores, -1e30)
    row_max = jnp.max(scores, axis=-1, keepdims=True)
    exponent = jnp.exp(scores - row_max)
    probs = exponent / jnp.sum(exponent, axis=-1, keepdims=True)
    probs_low = probs.astype(BF)
    attended = jnp.einsum("rhqk,rhkd->rhqd", probs_low, value, preferred_element_type=F32).astype(BF)

    part_of = HD // 2

    def to_out(v):
        if pairs:
            core = c.g % 2
            cuts = [v[:, k * part_of : (k + 1) * part_of] for k in range(2 * hl)]
            v = jnp.stack([jnp.concatenate(cuts[0::2], axis=1), jnp.concatenate(cuts[1::2], axis=1)])
            own, got = pick(v, core), c.swap_tokens(pick(v, 1 - core), 1)
            first = jnp.where(core == 0, own, got)
            second = jnp.where(core == 0, got, own)
            return jnp.concatenate([first, second], axis=1)
        v = v.reshape(toks, wide // (size * n_out), size, n_out)
        v = c.exchange(v.transpose(2, 0, 1, 3).reshape(size, toks, wide // size), True)
        return v.transpose(1, 0, 2).reshape(toks, wide)

    def from_out(v):
        if pairs:
            core = c.g % 2
            v = jnp.stack([v[:, : wide // 2], v[:, wide // 2 :]])
            own, got = pick(v, core), c.swap_tokens(pick(v, 1 - core), 1)
            halves = [jnp.where(core == 0, own, got), jnp.where(core == 0, got, own)]
            cuts = [u[:, k * part_of : (k + 1) * part_of] for k in range(hl) for u in halves]
            return jnp.concatenate(cuts, axis=1)
        v = c.exchange(v.reshape(toks, size, wide // size).transpose(1, 0, 2), True)
        v = v.reshape(size, toks, wide // (size * n_out), n_out).transpose(1, 2, 0, 3)
        return v.reshape(toks, wide)

    attended = to_out(by_tokens(attended))
    branch = c.scatter_tokens(attended, lambda v: dot_nn(v, full_out))
    branch_scale = lax.rsqrt(jnp.mean(branch * branch, axis=-1, keepdims=True) + eps)
    hidden = flat_in.astype(F32) + branch * branch_scale * norm_gains[2]
    hidden_low = c.gather_tokens(hidden.astype(BF))

    gate_up = dot_nn(hidden_low, full_gu)
    gate, up = gate_up[:, :ffl], gate_up[:, ffl:]
    sig = jax.nn.sigmoid(gate)
    inner = (gate * sig * up).astype(BF)
    branch2 = c.scatter_tokens(inner, lambda v: dot_nn(v, full_down))
    branch2_scale = lax.rsqrt(jnp.mean(branch2 * branch2, axis=-1, keepdims=True) + eps)
    output = (hidden + branch2 * branch2_scale * norm_gains[3]).astype(BF)

    upstream = cotangent.reshape(tl, d).astype(F32)
    grad_branch2, gain_mlp = norm_back(branch2, branch2_scale, norm_gains[3], upstream)
    grad_branch2 = c.gather_tokens(grad_branch2.astype(BF))
    g_down = dot_tn(inner, grad_branch2).astype(BF)
    sum_down = c.scatter(g_down)
    grad_inner = dot_nt(after(grad_branch2, g_down), full_down)
    grad_gate = grad_inner * up * sig * (1.0 + gate * (1.0 - sig))
    grad_gu = jnp.concatenate([grad_gate, grad_inner * (gate * sig)], axis=1).astype(BF)
    grad_hidden = upstream + c.scatter_tokens(grad_gu, lambda v: dot_nt(v, full_gu))
    g_gu = dot_tn(hidden_low, grad_gu).astype(BF)
    sum_gu = c.scatter(g_gu)
    grad_branch, gain_attn = norm_back(branch, branch_scale, norm_gains[2], grad_hidden)
    grad_branch = c.gather_tokens(grad_branch.astype(BF))
    grad_branch = after(grad_branch, sum_down)
    g_out = dot_tn(attended, grad_branch).astype(BF)
    sum_out = c.scatter(g_out)
    grad_att = by_rows(from_out(dot_nt(grad_branch, full_out).astype(BF)))
    grad_probs = jnp.einsum("rhqd,rhkd->rhqk", grad_att, value, preferred_element_type=F32)
    grad_value = jnp.einsum("rhqk,rhqd->rhkd", probs_low, grad_att, preferred_element_type=F32)
    row_sum = jnp.sum(probs * grad_probs, axis=-1, keepdims=True)
    grad_scores = (probs * (grad_probs - row_sum)).astype(BF)
    grad_query = jnp.einsum("rhqk,rhkd->rhqd", grad_scores, key, preferred_element_type=F32)
    grad_key = jnp.einsum("rhqk,rhqd->rhkd", grad_scores, query, preferred_element_type=F32)
    grad_query = (grad_query * score_scale).astype(BF).astype(F32)
    grad_key = (grad_key * score_scale).astype(BF).astype(F32)
    e_query = rotate(grad_query, cosine, sine_table, -1.0)
    e_key = rotate(grad_key, cosine, sine_table, -1.0)
    scaled_q, scaled_k = e_query * gain_q, e_key * gain_k
    sums = jnp.stack(
        [jnp.sum(scaled_q * query_pre, axis=(1, 3)), jnp.sum(scaled_k * key_pre, axis=(1, 3))]
    )
    mean_q, mean_k = stat_rows(c.sum_tokens(stat_tokens(sums)) / d)
    grad_qp = query_scale * scaled_q - query_pre * query_scale**3 * mean_q
    grad_kp = key_scale * scaled_k - key_pre * key_scale**3 * mean_k
    gain_query = jnp.sum(e_query * query_pre * query_scale, axis=(0, 2)).reshape(wide)
    gain_key = jnp.sum(e_key * key_pre * key_scale, axis=(0, 2)).reshape(wide)
    own_terms = jnp.zeros((size, 2, wide), F32)
    own_terms = lax.dynamic_update_slice(own_terms, jnp.stack([gain_query, gain_key])[None], (c.g, 0, 0))
    if pairs:
        own_terms = own_terms.reshape(half_group, 2, 2, hl, HD).transpose(2, 1, 3, 0, 4)
    else:
        own_terms = own_terms.transpose(1, 0, 2)
    terms = jnp.concatenate([own_terms.reshape(2, d), jnp.stack([gain_attn, gain_mlp])])
    grad_gains = c.sum_all(terms)
    grad_mixed = by_tokens(
        jnp.concatenate([grad_qp.astype(BF), grad_kp.astype(BF), grad_value.astype(BF)], axis=1)
    )
    back_gu = c.exchange_pair(sum_gu.reshape(size, n_in, 2 * ffl), c.swap)
    grad_mixed = after(grad_mixed, back_gu, grad_gains)
    g_qkv = dot_tn(x_full, grad_mixed).astype(BF)
    sum_qkv = c.scatter(g_qkv)
    back_gu = c.exchange_chips(back_gu, c.swap)
    grad_mixed = after(grad_mixed, g_qkv, back_gu)
    grad_input = grad_hidden + c.scatter_tokens(grad_mixed, lambda v: dot_nt(v, full_qkv))
    back_gu = back_gu.astype(F32).reshape(size, n_in, 2, copies, n_ff)
    grad_gate_up = back_gu.transpose(1, 2, 3, 0, 4)
    sum_qkv = after(sum_qkv, grad_gate_up)
    back_qkv = c.exchange(sum_qkv.reshape(size, n_in, 3 * wide)).astype(F32)
    if pairs:
        grad_qkv = back_qkv.reshape(half_group, 2, n_in, 3, hl, HD).transpose(2, 3, 1, 4, 0, 5)
    else:
        grad_qkv = back_qkv.reshape(size, n_in, 3, wide).transpose(1, 2, 0, 3)

    return (
        output.reshape(layer_input.shape),
        grad_input.reshape(layer_input.shape),
        grad_qkv.reshape(w_qkv.shape),
        sum_out.astype(F32),
        grad_gate_up.reshape(w_gate_up.shape),
        sum_down.astype(F32),
        grad_gains,
    )


def solution(mesh):
    both = P(("rows", "seq"), None)
    tokens = P("rows", "seq", None)
    return jax.shard_map(
        per_device,
        mesh=mesh,
        in_specs=(tokens, P("rows", None), both, both, both, both, P(), tokens),
        out_specs=(tokens, tokens, both, both, both, both, P()),
        check_vma=False,
    )
```
